256 devices in a mesh: seq: 16 (over x, y_hi, core), fsdp: 16 (over z, y_lo).
Axes of the slice: x: 4, y: 4 (y_hi: 2, y_lo: 2; y = y_hi * 2 + y_lo), z: 8, core: 2. Of those that a mesh axis runs over, the one named last changes fastest.
Arguments:
- hidden: bfloat16 [32768, 8192], P(('seq', 'fsdp')), may hold values from -24 to 24
- kv_blocks: bfloat16 [8192, 1024], P('fsdp'), may hold values from -0.0625 to 0.0625
- kv_scale: float32 [64, 8], P('fsdp'), may hold values from 0.5 to 2
- queries: bfloat16 [32768, 4096], P(('seq', 'fsdp')), may hold values from -24 to 24
- grad_out: bfloat16 [32768, 4096], P(('seq', 'fsdp')), may hold values from -6 to 6
Outputs:
- attn_out: bfloat16 [32768, 4096], P(('seq', 'fsdp'))
- grad_queries: bfloat16 [32768, 4096], P(('seq', 'fsdp'))
- grad_hidden: bfloat16 [32768, 8192], P(('seq', 'fsdp'))
- weight_grad: float32 [8192, 1024], P('fsdp')
The draws below stay inside these ranges and needn't reach their ends.
All inputs are finite; a program needn't handle non-finite values.
Results may differ from the reference program's by a relative error of at most 0.0075.
The reference program's roundings to bfloat16 on the way (of `weights`, `kv`, `probs_b` and `dscores`) count: a program that leaves them out, or rounds other values in their place, can miss the bound.
Values may be sent and summed in bfloat16 or wider, within the bound.
No kernel may reach another device: no remote copies, remote signals or barrier semaphores. Data moves between devices by JAX's collectives and lax.ppermute only.
A program may use at most 128 MiB of HBM per device.

```python
import math
import jax
import jax.numpy as jnp
from jax import lax

D = 8192
HEADS = 32
KV_HEADS = 4
HEAD = 128
QB = 128
TOK_DEV = 128
KVW = 512
SEG = 2048
SPAN = 1024
TOKENS = 32768


def draw_queries(key, part):
    shape = (TOKENS, HEADS * HEAD)
    first = jax.random.fold_in(jax.random.fold_in(key, 17), 0)
    return jnp.clip(jax.random.normal(first, shape, jnp.float32), -4.0, 4.0).astype(jnp.bfloat16)


def strengthened(array, rng, source, target, blocks, factor):
    def block_of(axis_at):
        return (jnp.arange(array.shape[axis_at]) // (array.shape[axis_at] // blocks)).reshape((-1,) + (1,) * (array.ndim - 1 - axis_at))

    first = jax.random.permutation(rng, blocks)[block_of(target)]
    far = (block_of(target) + blocks // 2) % blocks
    return jnp.where((block_of(source) == first) | (block_of(source) == far), factor * array, array)


def shard_levels(own_key, shape, cuts, low, top_value):
    gain, own = 1.0, jax.random.fold_in(own_key, 6)
    for axis_at, shards_of in cuts:
        draws = jnp.exp(jax.random.uniform(jax.random.fold_in(own, axis_at), (shards_of,), jnp.float32, low / len(cuts), top_value / len(cuts)))
        gain = gain * jnp.repeat(draws, shape[axis_at] // shards_of).reshape([-1 if axis == axis_at else 1 for axis in range(len(shape))])
    return gain


def centred(key, shape, scale, bound, shards=(), held_as=jnp.bfloat16):
    entries = jax.random.normal(key, shape, jnp.float32) * scale
    if len(shards) > 0:
        entries = shard_levels(key, shape, shards, -0.22, 0.18) * entries
    return jnp.clip(entries, min=-bound, max=bound).astype(held_as)


def noise_with(rng, shape, scale, bound, cuts, heavy, kind=jnp.bfloat16):
    entries = scale * jax.random.normal(rng, shape, jnp.float32)
    if cuts:
        entries = entries * shard_levels(rng, shape, cuts, -0.22, 0.18)
    return jnp.clip(strengthened(entries, jax.random.fold_in(rng, 3), *heavy), -bound, bound).astype(kind)


def setup_inputs(seed: int = 0) -> dict:
    key_list = jax.random.split(jax.random.key(seed), 6)
    return {
        "hidden": noise_with(key_list[0], (TOKENS, D), 1.0, 24.0, ((0, 256),), (0, 1, 256, 6.0)),
        "kv_blocks": centred(key_list[1], (D, 2 * KVW), D ** -0.5, 0.0625, ((0, 16),)),
        "kv_scale": jnp.clip(jnp.exp(math.log(2.0) - 1.3862944 * jax.random.uniform(key_list[2], (D // QB, 2 * KVW // QB), jnp.float32) ** shard_levels(key_list[2], (D // QB, 2 * KVW // QB), ((0, 16),), -0.2, 0.2)), 0.5, 2.0),
        "queries": draw_queries(jax.random.fold_in(key_list[5], 71), 0),
        "grad_out": centred(key_list[4], (TOKENS, HEADS * HEAD), 1.0, 6.0, ((0, 256),)),
    }


NEG = -1e+30

def dequantize(blocks, scale):
    rows, cols = blocks.shape
    grid = blocks.astype(jnp.float32).reshape(scale.shape[0], QB, scale.shape[1], QB)
    return (grid * scale[:, None, :, None]).reshape(rows, cols).astype(jnp.bfloat16)

def attend_group(operands, allowed):
    qgrp, kgrp, vgrp, ggrp = operands
    factor = 1.0 / math_sqrt(HEAD)
    qf = qgrp.astype(jnp.float32)
    kf = kgrp.astype(jnp.float32)
    vf = vgrp.astype(jnp.float32)
    gf = ggrp.astype(jnp.float32)
    scores = jnp.einsum('rhd,kd->rhk', qf, kf) * factor
    scores = jnp.where(allowed[:, None, :], scores, NEG)
    top = lax.optimization_barrier(jnp.max(scores, axis=-1, keepdims=True))
    expd = jnp.exp(scores - top)
    probs = expd / lax.optimization_barrier(jnp.sum(expd, axis=-1, keepdims=True))
    probs_b = probs.astype(jnp.bfloat16)
    pf = probs_b.astype(jnp.float32)
    output = jnp.einsum('rhk,kd->rhd', pf, vf).astype(jnp.bfloat16)
    dprobs = jnp.einsum('rhd,kd->rhk', gf, vf)
    delta = lax.optimization_barrier(jnp.sum(probs * dprobs, axis=-1, keepdims=True))
    dscores = (probs * (dprobs - delta) * factor).astype(jnp.bfloat16)
    df = dscores.astype(jnp.float32)
    gradq = jnp.einsum('rhk,kd->rhd', df, kf).astype(jnp.bfloat16)
    gradk = jnp.einsum('rhk,rhd->kd', df, qf)
    gradv = jnp.einsum('rhk,rhd->kd', pf, gf)
    return (output, gradq, gradk, gradv)

def math_sqrt(value):
    return float(value) ** 0.5

def attend(queries, window, grad_out, allowed):
    rows = queries.shape[0]
    count = window.shape[0]
    group = HEADS // KV_HEADS
    qgrp = queries.reshape(rows, KV_HEADS, group, HEAD).transpose(1, 0, 2, 3)
    ggrp = grad_out.reshape(rows, KV_HEADS, group, HEAD).transpose(1, 0, 2, 3)
    kgrp = window[:, :KVW].reshape(count, KV_HEADS, HEAD).transpose(1, 0, 2)
    vgrp = window[:, KVW:].reshape(count, KV_HEADS, HEAD).transpose(1, 0, 2)
    output, gradq, gradk, gradv = lax.map(lambda ops: attend_group(ops, allowed), (qgrp, kgrp, vgrp, ggrp))
    output = output.transpose(1, 0, 2, 3).reshape(rows, HEADS * HEAD)
    gradq = gradq.transpose(1, 0, 2, 3).reshape(rows, HEADS * HEAD)
    gradk = gradk.transpose(1, 0, 2).reshape(count, KVW)
    gradv = gradv.transpose(1, 0, 2).reshape(count, KVW)
    return (output, gradq, jnp.concatenate([gradk, gradv], axis=1))

def reference(hidden, kv_blocks, kv_scale, queries, grad_out):
    weights = dequantize(kv_blocks, kv_scale)
    kv = jnp.dot(hidden, weights, preferred_element_type=jnp.float32).astype(jnp.bfloat16)
    padded = jnp.concatenate([jnp.zeros((SPAN, 2 * KVW), jnp.bfloat16), kv], axis=0)
    width = SPAN + TOK_DEV
    blocks = TOKENS // TOK_DEV

    def step(carry, index):
        acc_all, acc_seg = carry
        start = (index * TOK_DEV).astype(jnp.int32)
        qrows = lax.dynamic_slice_in_dim(queries, start, TOK_DEV, 0)
        grows = lax.dynamic_slice_in_dim(grad_out, start, TOK_DEV, 0)
        window = lax.dynamic_slice_in_dim(padded, start, width, 0)
        qpos = start + jnp.arange(TOK_DEV, dtype=jnp.int32)
        kpos = start - SPAN + jnp.arange(width, dtype=jnp.int32)
        allowed = (qpos[:, None] - kpos[None, :] < SPAN) & (kpos[None, :] <= qpos[:, None]) & (kpos[None, :] >= 0)
        seg_start = start // SEG * SEG
        inside = (kpos >= seg_start).astype(jnp.float32)
        output, gradq, dwin = attend(qrows, window, grows, allowed)
        old_all = lax.dynamic_slice_in_dim(acc_all, start, width, 0)
        acc_all = lax.dynamic_update_slice_in_dim(acc_all, old_all + dwin, start, 0)
        old_seg = lax.dynamic_slice_in_dim(acc_seg, start, width, 0)
        acc_seg = lax.dynamic_update_slice_in_dim(acc_seg, old_seg + dwin * inside[:, None], start, 0)
        return ((acc_all, acc_seg), (output, gradq))
    zeros = jnp.zeros((SPAN + TOKENS, 2 * KVW), jnp.float32)
    (acc_all, acc_seg), (outputs, gradqs) = lax.scan(step, (zeros, zeros), jnp.arange(blocks, dtype=jnp.int32))
    attn_out = outputs.reshape(TOKENS, HEADS * HEAD)
    grad_queries = gradqs.reshape(TOKENS, HEADS * HEAD)
    dkv_all = acc_all[SPAN:].astype(jnp.bfloat16)
    dkv_seg = acc_seg[SPAN:].astype(jnp.bfloat16)
    grad_hidden = jnp.dot(dkv_seg, weights.T, preferred_element_type=jnp.float32).astype(jnp.bfloat16)
    weight_grad = jnp.dot(hidden.T, dkv_all, preferred_element_type=jnp.float32)
    return (attn_out, grad_queries, grad_hidden, weight_grad)
```

```python
import functools

import jax
import jax.numpy as jnp
from jax import lax
from jax.experimental import pallas as pl
from jax.experimental.pallas import tpu as pltpu
from jax.sharding import Mesh
from jax.sharding import PartitionSpec as P

HEADS = 32
KV_HEADS = 4
HEAD = 128
QB = 128
SPAN = 1024
AXES = ("x", "yh", "core", "zh", "zl", "yl")
SIZES = (4, 2, 2, 4, 2, 2)
FSDP = ("zh", "zl", "yl")
GROUP = ("zl", "yl")
PLANE = ("x", "yh")
MEMBERS = 4

FACTOR = 1.0 / float(HEAD) ** 0.5
LOG2E = 1.4426950408889634
NEG = -1e30
F32 = jnp.float32
BF16 = jnp.bfloat16


def nt(a, b):
    return lax.dot_general(a, b, (((1,), (1,)), ((), ())), preferred_element_type=F32)


def nn(a, b):
    return lax.dot_general(a, b, (((1,), (0,)), ((), ())), preferred_element_type=F32)


def tn(a, b):
    return lax.dot_general(a, b, (((0,), (0,)), ((), ())), preferred_element_type=F32)


def shifted(block, axes, distance):
    devices = range(lax.axis_size(axes))
    route = [(i - distance, i) for i in devices if i - distance in devices]
    return lax.ppermute(block, axes, route)


def rotated(block, axis, distance):
    size = lax.axis_size(axis)
    return lax.ppermute(block, axis, [(i, (i + distance) % size) for i in range(size)])


def swapped(block, axes, mask):
    return lax.ppermute(block, axes, [(i, i ^ mask) for i in range(lax.axis_size(axes))])


def exchange(blocks, axes):
    return lax.all_to_all(blocks, axes, split_axis=0, concat_axis=0, tiled=True)


def dequantize(blocks, scale):
    rows, cols = blocks.shape
    grid = blocks.astype(F32).reshape(scale.shape[0], QB, scale.shape[1], QB)
    return (grid * scale[:, None, :, None]).reshape(rows, cols).astype(BF16)


def project_kernel(h_ref, w_ref, o_ref):
    o_ref[0] = nn(h_ref[...], w_ref[...])


def project(hidden, weights):
    rows, depth = hidden.shape
    width = weights.shape[1] // MEMBERS
    return pl.pallas_call(
        project_kernel,
        grid=(MEMBERS,),
        in_specs=[
            pl.BlockSpec((rows, depth), lambda h: (0, 0)),
            pl.BlockSpec((depth, width), lambda h: (0, h)),
        ],
        out_specs=pl.BlockSpec((1, rows, width), lambda h: (h, 0, 0)),
        out_shape=jax.ShapeDtypeStruct((MEMBERS, rows, width), F32),
        compiler_params=pltpu.CompilerParams(vmem_limit_bytes=32 << 20),
        cost_estimate=pl.CostEstimate(
            flops=2 * rows * depth * width * MEMBERS, bytes_accessed=8 << 20, transcendentals=0
        ),
        name="project",
    )(hidden, weights)


def attention_kernel(
    lim_ref, q_ref, g_ref, far_ref, near_ref, own_ref,
    out_ref, dfar_ref, dnear_ref, down_ref, kv, acc,
):
    t = pl.program_id(0)
    group = own_ref.shape[0]
    tok = q_ref.shape[2]
    pairs = q_ref.shape[3] // (2 * HEAD)
    width = SPAN + tok

    @pl.when(t == 0)
    def _():
        kv[0:group] = far_ref[...]
        kv[group : 2 * group] = near_ref[...]
        kv[2 * group :] = own_ref[...]
        acc[...] = jnp.zeros_like(acc)

    start = pl.multiple_of(t * tok, tok)
    lim = lim_ref[t]

    def run(masked):
        keys = kv[pl.ds(start, width), 0:HEAD]
        vals = kv[pl.ds(start, width), HEAD : 2 * HEAD]
        row = lax.broadcasted_iota(jnp.int32, (tok, 2 * tok), 0)
        col = lax.broadcasted_iota(jnp.int32, (tok, 2 * tok), 1) & (tok - 1)
        for pair in range(pairs):
            a = slice(2 * pair * HEAD, (2 * pair + 1) * HEAD)
            b = slice((2 * pair + 1) * HEAD, (2 * pair + 2) * HEAD)
            q2 = jnp.concatenate([q_ref[0, 0, :, a], q_ref[0, 0, :, b]], axis=0)
            g2 = jnp.concatenate([g_ref[0, 0, :, a], g_ref[0, 0, :, b]], axis=0)
            s = nt(keys, q2)
            s = jnp.concatenate(
                [
                    jnp.where(row > col, s[:tok], NEG),
                    s[tok:SPAN],
                    jnp.where(row <= col, s[SPAN:], NEG),
                ],
                axis=0,
            )
            if masked:
                s = jnp.where(lax.broadcasted_iota(jnp.int32, s.shape, 0) >= lim, s, NEG)
            top = jnp.max(s, axis=0, keepdims=True) * (FACTOR * LOG2E)
            expd = jnp.exp2(s * (FACTOR * LOG2E) - top)
            probs = expd * (1.0 / jnp.sum(expd, axis=0, keepdims=True))
            probs_b = probs.astype(BF16)
            dprobs = nt(vals, g2)
            delta = jnp.sum(probs * dprobs, axis=0, keepdims=True)
            dscores = (probs * (dprobs - delta) * FACTOR).astype(BF16)
            acc[pl.ds(start, width), 0:HEAD] += nn(dscores, q2)
            acc[pl.ds(start, width), HEAD : 2 * HEAD] += nn(probs_b, g2)
            output = tn(probs_b, vals).astype(BF16)
            gradq = tn(dscores, keys).astype(BF16)
            out_ref[0, 0, :, a] = output[:tok]
            out_ref[0, 0, :, b] = output[tok:]
            out_ref[0, 1, :, a] = gradq[:tok]
            out_ref[0, 1, :, b] = gradq[tok:]

    @pl.when(lim <= 0)
    def _():
        run(False)

    @pl.when(lim > 0)
    def _():
        run(True)

    @pl.when(t == pl.num_programs(0) - 1)
    def _():
        dfar_ref[...] = acc[0:group].astype(dfar_ref.dtype)
        dnear_ref[...] = acc[group : 2 * group].astype(dnear_ref.dtype)
        down_ref[...] = acc[2 * group :]


def attention(lim, queries, far, near, own):
    steps, _, tok, cols = queries.shape
    group, both = own.shape
    whole = pl.BlockSpec((group, both), lambda t, lim: (0, 0))
    return pl.pallas_call(
        attention_kernel,
        grid_spec=pltpu.PrefetchScalarGridSpec(
            num_scalar_prefetch=1,
            grid=(steps,),
            in_specs=[
                pl.BlockSpec((1, 1, tok, cols), lambda t, lim: (t, 0, 0, 0)),
                pl.BlockSpec((1, 1, tok, cols), lambda t, lim: (t, 1, 0, 0)),
                whole,
                whole,
                whole,
            ],
            out_specs=[
                pl.BlockSpec((1, 2, tok, cols), lambda t, lim: (t, 0, 0, 0)),
                whole,
                whole,
                whole,
            ],
            scratch_shapes=[
                pltpu.VMEM((3 * group, both), BF16),
                pltpu.VMEM((3 * group, both), F32),
            ],
        ),
        out_shape=[
            jax.ShapeDtypeStruct(queries.shape, BF16),
            jax.ShapeDtypeStruct(own.shape, BF16),
            jax.ShapeDtypeStruct(own.shape, BF16),
            jax.ShapeDtypeStruct(own.shape, F32),
        ],
        compiler_params=pltpu.CompilerParams(vmem_limit_bytes=48 << 20),
        cost_estimate=pl.CostEstimate(
            flops=30_000_000_000, bytes_accessed=6 << 20, transcendentals=5_000_000
        ),
        name="attention",
    )(lim, queries, queries, far, near, own)


def grad_hidden_kernel(member_ref, d0, d1, d2, d3, w_ref, o_ref):
    total = None
    for k, d in enumerate((d0, d1, d2, d3)):
        width = d.shape[1]
        at = pl.multiple_of((member_ref[0] ^ k) * width, width)
        term = nt(d[...], w_ref[:, pl.ds(at, width)])
        total = term if total is None else total + term
    o_ref[...] = total.astype(BF16)


def grad_hidden_quarter(member, pieces, weights):
    rows, width = pieces[0].shape
    depth, cols = weights.shape
    step = 256
    piece = pl.BlockSpec((rows, width), lambda i, m: (0, 0))
    return pl.pallas_call(
        grad_hidden_kernel,
        grid_spec=pltpu.PrefetchScalarGridSpec(
            num_scalar_prefetch=1,
            grid=(depth // step,),
            in_specs=[piece] * 4 + [pl.BlockSpec((step, cols), lambda i, m: (i, 0))],
            out_specs=pl.BlockSpec((rows, step), lambda i, m: (0, i)),
        ),
        out_shape=jax.ShapeDtypeStruct((rows, depth), BF16),
        compiler_params=pltpu.CompilerParams(vmem_limit_bytes=32 << 20),
        cost_estimate=pl.CostEstimate(
            flops=2 * rows * depth * cols, bytes_accessed=8 << 20, transcendentals=0
        ),
        name="grad_hidden",
    )(member, *pieces, weights)


def weight_grad_kernel(place_ref, c0, c1, c2, c3, d_ref, o_ref):
    zh = place_ref[0]
    total = None
    for k, c in enumerate((c0, c1, c2, c3)):
        term = nn(c[...], d_ref[(zh - k) & 3, 0, 0])
        total = term if total is None else total + term
    h = pl.program_id(0)
    half = o_ref.shape[1] // 2
    at = pl.multiple_of(h * HEAD, HEAD)
    o_ref[:, pl.ds(at, HEAD)] = total[:, :HEAD]
    o_ref[:, pl.ds(half + at, HEAD)] = total[:, HEAD:]


def weight_grad_share(place, columns, gathered):
    feats, rows = columns[0].shape
    blocks = gathered.shape[0]
    both = gathered.shape[4]
    piece = pl.BlockSpec((feats, rows), lambda h, p: (0, 0))
    return pl.pallas_call(
        weight_grad_kernel,
        grid_spec=pltpu.PrefetchScalarGridSpec(
            num_scalar_prefetch=1,
            grid=(KV_HEADS,),
            in_specs=[piece] * 4
            + [
                pl.BlockSpec(
                    (blocks, 1, 1, rows, both), lambda h, p: (0, h // 2, (h % 2) ^ p[1], 0, 0)
                )
            ],
            out_specs=pl.BlockSpec((feats, both * KV_HEADS), lambda h, p: (0, 0)),
        ),
        out_shape=jax.ShapeDtypeStruct((feats, both * KV_HEADS), F32),
        compiler_params=pltpu.CompilerParams(vmem_limit_bytes=32 << 20),
        cost_estimate=pl.CostEstimate(
            flops=2 * feats * rows * blocks * both * KV_HEADS,
            bytes_accessed=8 << 20,
            transcendentals=0,
        ),
        name="weight_grad",
    )(place, *columns, gathered)


def body(hidden, kv_blocks, kv_scale, queries, grad_out):
    tok, depth = hidden.shape
    shard = kv_blocks.shape[0]
    half = shard // 2
    kv_cols = kv_blocks.shape[1]
    group = MEMBERS * tok
    zh = lax.axis_index("zh")
    core = lax.axis_index("core")
    yl = lax.axis_index("yl")
    member = lax.axis_index(GROUP)
    zhs = lax.axis_size("zh")

    blocks = lax.dynamic_slice_in_dim(kv_blocks, core * half, half, 0)
    scale = lax.dynamic_slice_in_dim(kv_scale, core * (half // QB), half // QB, 0)
    rows = dequantize(blocks, scale)
    rows = rows.reshape(half, 2, KV_HEADS, HEAD).transpose(0, 2, 1, 3).reshape(half, kv_cols)
    weights = lax.all_gather(rows, ("core", "zh"), axis=0, tiled=True)

    quarters = (
        hidden.reshape(tok, zhs, MEMBERS, 2, half).transpose(2, 0, 3, 1, 4).reshape(group, -1)
    )
    quarter = exchange(quarters, GROUP)

    pieces = jnp.stack(
        [
            queries.reshape(tok, MEMBERS, -1).transpose(1, 0, 2),
            grad_out.reshape(tok, MEMBERS, -1).transpose(1, 0, 2),
        ],
        axis=1,
    )
    heads = exchange(pieces, GROUP)

    partial = exchange(project(quarter, weights), GROUP)
    own = jnp.sum(partial, axis=0).astype(BF16)
    far = shifted(own, AXES, 2 * MEMBERS)
    near = shifted(own, AXES, MEMBERS)

    first = lax.axis_index(AXES) // MEMBERS * MEMBERS
    lim = jnp.maximum(0, SPAN - (first + jnp.arange(MEMBERS, dtype=jnp.int32)) * tok)

    far, near, quarter = lax.optimization_barrier((far, near, quarter))
    grid = quarter.reshape(group, 2, zhs, half)
    columns = []
    for k in range(zhs):
        to = (zh + k) % zhs
        block = lax.dynamic_slice_in_dim(grid, to, 1, 2).reshape(group, shard)
        columns.append(rotated(block, "zh", k) if k else block)

    out, dfar, dnear, down = attention(lim, heads, far, near, own)
    from_far = shifted(dfar, AXES, -2 * MEMBERS).astype(F32)
    from_near = shifted(dnear, AXES, -MEMBERS).astype(F32)
    all_grad = (down + from_near + from_far).astype(BF16)
    inside = down + jnp.where(zh + 1 < zhs, from_near, 0.0) + jnp.where(zh + 2 < zhs, from_far, 0.0)
    seg_grad = inside.astype(BF16)

    other = swapped(all_grad, "yl", 1)
    pair = jnp.stack([all_grad, other], axis=0)[None]
    gathered = lax.all_gather(pair, ("zh", "zl"), axis=0, tiled=True)
    gathered = gathered.reshape(zhs, 2, 2, group, -1)

    out, seg_grad, _ = lax.optimization_barrier((out, seg_grad, pair))
    turned = [c.T for c in columns]
    segs = [seg_grad] + [swapped(seg_grad, GROUP, k) for k in (1, 2, 3)]
    back = exchange(grad_hidden_quarter(member.reshape(1), segs, weights), GROUP)
    grad_hidden = (
        back.reshape(MEMBERS, tok, 2, zhs, half).transpose(1, 3, 0, 2, 4).reshape(tok, depth)
    )
    out = exchange(out, GROUP)
    attn_out = out[:, 0].transpose(1, 0, 2).reshape(tok, -1)
    grad_queries = out[:, 1].transpose(1, 0, 2).reshape(tok, -1)

    share = weight_grad_share(jnp.stack([zh, yl]).astype(jnp.int32), turned, gathered)
    mine = lax.dynamic_slice_in_dim(share, core * half, half, 0)
    theirs = lax.dynamic_slice_in_dim(share, (1 - core) * half, half, 0)
    mine = mine + swapped(theirs, "core", 1)
    planes = lax.axis_size(PLANE)
    parts = exchange(mine.reshape(planes, half // planes, kv_cols), PLANE)
    summed = jnp.sum(parts, axis=0)
    spread = exchange(jnp.broadcast_to(summed[None], parts.shape), PLANE).reshape(half, kv_cols)
    opposite = swapped(spread, "core", 1)
    weight_grad = jnp.where(
        core == 0,
        jnp.concatenate([spread, opposite], axis=0),
        jnp.concatenate([opposite, spread], axis=0),
    )
    return (attn_out, grad_queries, grad_hidden, weight_grad)


def solution(mesh):
    finer = Mesh(mesh.devices.reshape(SIZES), AXES)
    placed = (P(AXES, None), P(FSDP, None), P(FSDP, None), P(AXES, None), P(AXES, None))
    return jax.shard_map(
        body,
        mesh=finer,
        in_specs=placed,
        out_specs=(P(AXES, None), P(AXES, None), P(AXES, None), P(FSDP, None)),
        check_vma=False,
    )
```

```python
import functools

import jax
import jax.numpy as jnp
from jax import lax
from jax.experimental import pallas as pl
from jax.experimental.pallas import tpu as pltpu
from jax.sharding import Mesh
from jax.sharding import PartitionSpec as P

HEADS = 32
KV_HEADS = 4
HEAD = 128
QB = 128
SPAN = 1024
AXES = ("x", "yh", "core", "zh", "zl", "yl")
SIZES = (4, 2, 2, 4, 2, 2)
FSDP = ("zh", "zl", "yl")
GROUP = ("zl", "yl")
PLANE = ("x", "yh")
MEMBERS = 4

FACTOR = 1.0 / float(HEAD) ** 0.5
LOG2E = 1.4426950408889634
NEG = -1e30
F32 = jnp.float32
BF16 = jnp.bfloat16


def nt(a, b):
    return lax.dot_general(a, b, (((1,), (1,)), ((), ())), preferred_element_type=F32)


def nn(a, b):
    return lax.dot_general(a, b, (((1,), (0,)), ((), ())), preferred_element_type=F32)


def tn(a, b):
    return lax.dot_general(a, b, (((0,), (0,)), ((), ())), preferred_element_type=F32)


def shifted(block, axes, distance):
    devices = range(lax.axis_size(axes))
    route = [(i - distance, i) for i in devices if i - distance in devices]
    return lax.ppermute(block, axes, route)


def swapped(block, axes, mask):
    return lax.ppermute(block, axes, [(i, i ^ mask) for i in range(lax.axis_size(axes))])


def fanned(block):
    return [block] + [swapped(block, GROUP, k) for k in range(1, MEMBERS)]


def dealt(blocks):
    return [blocks[0]] + [swapped(blocks[k], GROUP, k) for k in range(1, MEMBERS)]


def exchange(blocks, axes):
    return lax.all_to_all(blocks, axes, split_axis=0, concat_axis=0, tiled=True)


def small(name, grid, in_specs, out_specs, out_shape, kernel, prefetch=0):
    return pl.pallas_call(
        kernel,
        grid_spec=pltpu.PrefetchScalarGridSpec(
            num_scalar_prefetch=prefetch, grid=grid, in_specs=in_specs, out_specs=out_specs
        ),
        out_shape=out_shape,
        compiler_params=pltpu.CompilerParams(vmem_limit_bytes=16 << 20),
        cost_estimate=pl.CostEstimate(flops=0, bytes_accessed=4 << 20, transcendentals=0),
        name=name,
    )


def dequantize_kernel(core_ref, b_ref, s_ref, o_ref):
    del core_ref
    for i in range(b_ref.shape[0] // QB):
        for j in range(b_ref.shape[1] // QB):
            to = (j % KV_HEADS) * 2 + j // KV_HEADS
            block = b_ref[i * QB : (i + 1) * QB, j * QB : (j + 1) * QB].astype(F32)
            scale = s_ref[0, i : i + 1, j : j + 1]
            o_ref[i * QB : (i + 1) * QB, to * QB : (to + 1) * QB] = (block * scale).astype(BF16)


def dequantize(core, blocks, scale):
    rows, cols = blocks.shape
    half = rows // 2
    scale = scale.reshape(2, half // QB, cols // QB)
    return small(
        "dequantize",
        (1,),
        [
            pl.BlockSpec((half, cols), lambda i, c: (c[0], 0)),
            pl.BlockSpec((1,) + scale.shape[1:], lambda i, c: (c[0], 0, 0)),
        ],
        pl.BlockSpec((half, cols), lambda i, c: (0, 0)),
        jax.ShapeDtypeStruct((half, cols), BF16),
        dequantize_kernel,
        1,
    )(core, blocks, scale)


def pack_hidden_kernel(*refs):
    o_ref = refs[-1]
    zhs = len(refs) - 1
    half = refs[0].shape[1] // 2
    for zh, ref in enumerate(refs[:-1]):
        for core in range(2):
            at = (core * zhs + zh) * half
            o_ref[0, :, at : at + half] = ref[:, core * half : (core + 1) * half]


def pack_hidden(hidden, zhs):
    tok, depth = hidden.shape
    quarter = depth // MEMBERS
    piece = quarter // zhs
    return small(
        "pack_hidden",
        (MEMBERS,),
        [pl.BlockSpec((tok, piece), lambda m, z=z: (0, z * MEMBERS + m)) for z in range(zhs)],
        pl.BlockSpec((1, tok, quarter), lambda m: (m, 0, 0)),
        jax.ShapeDtypeStruct((MEMBERS, tok, quarter), hidden.dtype),
        pack_hidden_kernel,
    )(*[hidden] * zhs)


def unpack_hidden_kernel(member_ref, *refs):
    o_ref = refs[-1]
    half = refs[0].shape[1]
    for k in range(MEMBERS):
        for core in range(2):
            at = (2 * (member_ref[0] ^ k) + core) * half
            o_ref[:, pl.ds(pl.multiple_of(at, half), half)] = refs[2 * k + core][...]


def unpack_hidden(member, pieces, zhs):
    tok, quarter = pieces[0].shape
    half = quarter // (2 * zhs)
    specs = [pl.BlockSpec((tok, half), lambda z, m, c=c: (0, c * zhs + z)) for c in range(2)]
    return small(
        "unpack_hidden",
        (zhs,),
        specs * MEMBERS,
        pl.BlockSpec((tok, 2 * half * MEMBERS), lambda z, m: (0, z)),
        jax.ShapeDtypeStruct((tok, quarter * MEMBERS), pieces[0].dtype),
        unpack_hidden_kernel,
        1,
    )(member, *[p for p in pieces for _ in range(2)])


def pack_heads_kernel(q_ref, g_ref, o_ref):
    o_ref[0, 0] = q_ref[...]
    o_ref[0, 1] = g_ref[...]


def pack_heads(queries, grad_out):
    tok, cols = queries.shape
    width = cols // MEMBERS
    block = pl.BlockSpec((tok, width), lambda m: (0, m))
    return small(
        "pack_heads",
        (MEMBERS,),
        [block, block],
        pl.BlockSpec((1, 2, tok, width), lambda m: (m, 0, 0, 0)),
        jax.ShapeDtypeStruct((MEMBERS, 2, tok, width), queries.dtype),
        pack_heads_kernel,
    )(queries, grad_out)


def unpack_heads_kernel(member_ref, *refs):
    a_ref, b_ref = refs[-2:]
    width = refs[0].shape[2]
    for k in range(MEMBERS):
        at = pl.ds(pl.multiple_of((member_ref[0] ^ k) * width, width), width)
        a_ref[:, at] = refs[k][0]
        b_ref[:, at] = refs[k][1]


def unpack_heads(member, pieces):
    _, tok, width = pieces[0].shape
    steps = 4
    rows = tok // steps
    block = pl.BlockSpec((rows, width * MEMBERS), lambda i, m: (i, 0))
    shape = jax.ShapeDtypeStruct((tok, width * MEMBERS), pieces[0].dtype)
    return small(
        "unpack_heads",
        (steps,),
        [pl.BlockSpec((2, rows, width), lambda i, m: (0, i, 0))] * MEMBERS,
        [block, block],
        [shape, shape],
        unpack_heads_kernel,
        1,
    )(member, *pieces)


def turn_kernel(x_ref, o_ref):
    o_ref[...] = x_ref[...].T


def turn(x):
    rows, cols = x.shape
    step = cols // 4
    return small(
        "turn",
        (4,),
        [pl.BlockSpec((rows, step), lambda i: (0, i))],
        pl.BlockSpec((step, rows), lambda i: (i, 0)),
        jax.ShapeDtypeStruct((cols, rows), x.dtype),
        turn_kernel,
    )(x)


def project_kernel(h_ref, w_ref, o_ref):
    o_ref[0] = nn(h_ref[...], w_ref[...])


def project(hidden, weights):
    rows, depth = hidden.shape
    width = weights.shape[1] // MEMBERS
    return pl.pallas_call(
        project_kernel,
        grid=(MEMBERS,),
        in_specs=[
            pl.BlockSpec((rows, depth), lambda h: (0, 0)),
            pl.BlockSpec((depth, width), lambda h: (0, h)),
        ],
        out_specs=pl.BlockSpec((1, rows, width), lambda h: (h, 0, 0)),
        out_shape=jax.ShapeDtypeStruct((MEMBERS, rows, width), F32),
        compiler_params=pltpu.CompilerParams(vmem_limit_bytes=56 << 20),
        cost_estimate=pl.CostEstimate(
            flops=2 * rows * depth * width * MEMBERS, bytes_accessed=8 << 20, transcendentals=0
        ),
        name="project",
    )(hidden, weights)


def attention_kernel(
    place_ref, q_ref, g_ref, far_ref, near_ref, own_ref,
    out_ref, dfar_ref, dnear_ref, down_ref, kv, acc,
):
    t = pl.program_id(0)
    group = own_ref.shape[0]
    tok = q_ref.shape[2]
    pairs = q_ref.shape[3] // (2 * HEAD)
    width = SPAN + tok

    @pl.when(t == 0)
    def _():
        kv[0:group] = far_ref[...]
        kv[group : 2 * group] = near_ref[...]
        kv[2 * group :] = own_ref[...]
        acc[...] = jnp.zeros_like(acc)

    start = pl.multiple_of(t * tok, tok)
    lim = place_ref[t + 1]

    def run(masked):
        keys = kv[pl.ds(start, width), 0:HEAD]
        vals = kv[pl.ds(start, width), HEAD : 2 * HEAD]
        row = lax.broadcasted_iota(jnp.int32, (tok, 2 * tok), 0)
        col = lax.broadcasted_iota(jnp.int32, (tok, 2 * tok), 1) & (tok - 1)
        for pair in range(pairs):
            a = slice(2 * pair * HEAD, (2 * pair + 1) * HEAD)
            b = slice((2 * pair + 1) * HEAD, (2 * pair + 2) * HEAD)
            q2 = jnp.concatenate([q_ref[0, 0, :, a], q_ref[0, 0, :, b]], axis=0)
            g2 = jnp.concatenate([g_ref[0, 0, :, a], g_ref[0, 0, :, b]], axis=0)
            s = nt(keys, q2)
            s = jnp.concatenate(
                [
                    jnp.where(row > col, s[:tok], NEG),
                    s[tok:SPAN],
                    jnp.where(row <= col, s[SPAN:], NEG),
                ],
                axis=0,
            )
            if masked:
                s = jnp.where(lax.broadcasted_iota(jnp.int32, s.shape, 0) >= lim, s, NEG)
            top = jnp.max(s, axis=0, keepdims=True) * (FACTOR * LOG2E)
            expd = jnp.exp2(s * (FACTOR * LOG2E) - top)
            probs = expd * (1.0 / jnp.sum(expd, axis=0, keepdims=True))
            probs_b = probs.astype(BF16)
            dprobs = nt(vals, g2)
            delta = jnp.sum(probs * dprobs, axis=0, keepdims=True)
            dscores = (probs * (dprobs - delta) * FACTOR).astype(BF16)
            acc[pl.ds(start, width), 0:HEAD] += nn(dscores, q2)
            acc[pl.ds(start, width), HEAD : 2 * HEAD] += nn(probs_b, g2)
            output = tn(probs_b, vals).astype(BF16)
            gradq = tn(dscores, keys).astype(BF16)
            out_ref[0, 0, :, a] = output[:tok]
            out_ref[0, 0, :, b] = output[tok:]
            out_ref[0, 1, :, a] = gradq[:tok]
            out_ref[0, 1, :, b] = gradq[tok:]

    @pl.when(lim <= 0)
    def _():
        run(False)

    @pl.when(lim > 0)
    def _():
        run(True)

    @pl.when(t == pl.num_programs(0) - 1)
    def _():
        dfar_ref[...] = acc[0:group].astype(dfar_ref.dtype)
        dnear_ref[...] = acc[group : 2 * group].astype(dnear_ref.dtype)
        down_ref[...] = acc[2 * group :]


def attention(place, queries, far, near, own):
    steps, _, tok, cols = queries.shape
    group, both = own.shape
    whole = pl.BlockSpec((group, both), lambda t, p: (0, 0))
    return pl.pallas_call(
        attention_kernel,
        grid_spec=pltpu.PrefetchScalarGridSpec(
            num_scalar_prefetch=1,
            grid=(steps,),
            in_specs=[
                pl.BlockSpec((1, 1, tok, cols), lambda t, p: (t, 0, 0, 0)),
                pl.BlockSpec((1, 1, tok, cols), lambda t, p: (t, 1, 0, 0)),
                whole,
                whole,
                whole,
            ],
            out_specs=[
                pl.BlockSpec((1, 2, tok, cols), lambda t, p: (t ^ p[0], 0, 0, 0)),
                whole,
                whole,
                whole,
            ],
            scratch_shapes=[
                pltpu.VMEM((3 * group, both), BF16),
                pltpu.VMEM((3 * group, both), F32),
            ],
        ),
        out_shape=[
            jax.ShapeDtypeStruct(queries.shape, BF16),
            jax.ShapeDtypeStruct(own.shape, BF16),
            jax.ShapeDtypeStruct(own.shape, BF16),
            jax.ShapeDtypeStruct(own.shape, F32),
        ],
        compiler_params=pltpu.CompilerParams(vmem_limit_bytes=48 << 20),
        cost_estimate=pl.CostEstimate(
            flops=30_000_000_000, bytes_accessed=6 << 20, transcendentals=5_000_000
        ),
        name="attention",
    )(place, queries, queries, far, near, own)


def grad_hidden_kernel(member_ref, d0, d1, d2, d3, w_ref, o_ref):
    total = None
    for k, d in enumerate((d0, d1, d2, d3)):
        width = d.shape[1]
        at = pl.multiple_of((member_ref[0] ^ k) * width, width)
        term = nt(d[...], w_ref[:, pl.ds(at, width)])
        total = term if total is None else total + term
    tok = o_ref.shape[1]
    for t in range(MEMBERS):
        o_ref[member_ref[0] ^ t] = total[t * tok : (t + 1) * tok].astype(BF16)


def grad_hidden_quarter(member, pieces, weights):
    rows, width = pieces[0].shape
    depth, cols = weights.shape
    step = 256
    piece = pl.BlockSpec((rows, width), lambda i, m: (0, 0))
    return pl.pallas_call(
        grad_hidden_kernel,
        grid_spec=pltpu.PrefetchScalarGridSpec(
            num_scalar_prefetch=1,
            grid=(depth // step,),
            in_specs=[piece] * 4 + [pl.BlockSpec((step, cols), lambda i, m: (i, 0))],
            out_specs=pl.BlockSpec((MEMBERS, rows // MEMBERS, step), lambda i, m: (0, 0, i)),
        ),
        out_shape=jax.ShapeDtypeStruct((MEMBERS, rows // MEMBERS, depth), BF16),
        compiler_params=pltpu.CompilerParams(vmem_limit_bytes=32 << 20),
        cost_estimate=pl.CostEstimate(
            flops=2 * rows * depth * cols, bytes_accessed=8 << 20, transcendentals=0
        ),
        name="grad_hidden",
    )(member, *pieces, weights)


def weight_grad_kernel(member_ref, h_ref, d0, d1, d2, d3, theirs_ref, mine_ref, *, steps):
    def run(o_ref):
        planes, _, rows, cols = o_ref.shape
        for k, d in enumerate((d0, d1, d2, d3)):
            at = pl.multiple_of((member_ref[0] ^ k) * HEAD, HEAD)
            term = nn(h_ref[...], d[...]).astype(o_ref.dtype).reshape(planes, rows, 2 * HEAD)
            o_ref[:, 0, :, pl.ds(at, HEAD)] = term[:, :, :HEAD]
            o_ref[:, 0, :, pl.ds(cols // 2 + at, HEAD)] = term[:, :, HEAD:]

    @pl.when(pl.program_id(0) < steps)
    def _():
        run(theirs_ref)

    @pl.when(pl.program_id(0) >= steps)
    def _():
        run(mine_ref)


def weight_grad_share(place, turned, pieces, steps, planes):
    feats, tokens = turned.shape
    both = pieces[0].shape[1]
    cols = both * KV_HEADS
    step = feats // (2 * steps)
    rows = step // planes

    def block(i, p):
        return (jnp.where(p[1] == 0, (i + steps) % (2 * steps), i), 0)

    piece = pl.BlockSpec((tokens, both), lambda i, p: (0, 0))
    out = (planes, 1, rows, cols)
    return pl.pallas_call(
        functools.partial(weight_grad_kernel, steps=steps),
        grid_spec=pltpu.PrefetchScalarGridSpec(
            num_scalar_prefetch=1,
            grid=(2 * steps,),
            in_specs=[pl.BlockSpec((step, tokens), block)] + [piece] * 4,
            out_specs=[
                pl.BlockSpec(out, lambda i, p: (0, jnp.minimum(i, steps - 1), 0, 0)),
                pl.BlockSpec(out, lambda i, p: (0, jnp.maximum(i - steps, 0), 0, 0)),
            ],
        ),
        out_shape=[
            jax.ShapeDtypeStruct((planes, steps, rows, cols), BF16),
            jax.ShapeDtypeStruct((planes, steps, rows, cols), F32),
        ],
        compiler_params=pltpu.CompilerParams(vmem_limit_bytes=32 << 20),
        cost_estimate=pl.CostEstimate(
            flops=2 * feats * tokens * cols, bytes_accessed=10 << 20, transcendentals=0
        ),
        name="weight_grad",
    )(place, turned, *pieces)


def body(hidden, kv_blocks, kv_scale, queries, grad_out):
    tok = hidden.shape[0]
    half = kv_blocks.shape[0] // 2
    kv_cols = kv_blocks.shape[1]
    zh = lax.axis_index("zh")
    core = lax.axis_index("core").reshape(1)
    member = lax.axis_index(GROUP).reshape(1)
    zhs = lax.axis_size("zh")
    planes = lax.axis_size(PLANE)

    rows = dequantize(core, kv_blocks, kv_scale)
    weights = lax.all_gather(rows, ("core", "zh"), axis=0, tiled=True)
    quarter = exchange(pack_hidden(hidden, zhs), GROUP).reshape(MEMBERS * tok, -1)
    heads = exchange(pack_heads(queries, grad_out), GROUP)

    weights, quarter, heads = lax.optimization_barrier((weights, quarter, heads))
    partial = exchange(project(quarter, weights), GROUP)
    own = jnp.sum(partial, axis=0).astype(BF16)
    far = shifted(own, AXES, 2 * MEMBERS)
    near = shifted(own, AXES, MEMBERS)
    quarter, own = lax.optimization_barrier((quarter, own))
    turned = turn(quarter)

    first = lax.axis_index(AXES) // MEMBERS * MEMBERS
    lim = jnp.maximum(0, SPAN - (first + jnp.arange(MEMBERS, dtype=jnp.int32)) * tok)
    far, near, turned = lax.optimization_barrier((far, near, turned))
    out, dfar, dnear, down = attention(
        jnp.concatenate([member, lim]).astype(jnp.int32), heads, far, near, own
    )
    from_far = shifted(dfar, AXES, -2 * MEMBERS).astype(F32)
    from_near = shifted(dnear, AXES, -MEMBERS).astype(F32)
    all_grad = (down + from_near + from_far).astype(BF16)
    inside = down + jnp.where(zh + 1 < zhs, from_near, 0.0) + jnp.where(zh + 2 < zhs, from_far, 0.0)
    seg_grad = inside.astype(BF16)

    alls = fanned(all_grad)
    place = jnp.concatenate([member, core]).astype(jnp.int32)
    theirs, mine = weight_grad_share(place, turned, alls, zhs, planes)

    out, seg_grad, theirs = lax.optimization_barrier((out, seg_grad, theirs))
    outs = dealt(out)
    segs = fanned(seg_grad)
    mine = (mine + swapped(theirs, "core", 1).astype(F32)).astype(BF16)
    mine, segs = lax.optimization_barrier((mine, segs))
    back = grad_hidden_quarter(member, segs, weights)
    parts = exchange(mine, PLANE)
    parts, outs, back = lax.optimization_barrier((parts, outs, back))
    backs = dealt(back)
    parts = jnp.sum(parts.astype(F32), axis=0)
    summed = jnp.sum(exchange(parts, "zh"), axis=0)
    spread = exchange(jnp.broadcast_to(summed[None], (planes,) + summed.shape), PLANE)
    backs, spread = lax.optimization_barrier((backs, spread))
    spread = spread.reshape(half, kv_cols)
    opposite = swapped(spread, "core", 1)
    attn_out, grad_queries = unpack_heads(member, outs)
    grad_hidden = unpack_hidden(member, backs, zhs)
    weight_grad = jnp.where(
        core[0] == 0,
        jnp.concatenate([spread, opposite], axis=0),
        jnp.concatenate([opposite, spread], axis=0),
    )
    return (attn_out, grad_queries, grad_hidden, weight_grad)


def solution(mesh):
    finer = Mesh(mesh.devices.reshape(SIZES), AXES)
    placed = (P(AXES, None), P(FSDP, None), P(FSDP, None), P(AXES, None), P(AXES, None))
    return jax.shard_map(
        body,
        mesh=finer,
        in_specs=placed,
        out_specs=(P(AXES, None), P(AXES, None), P(AXES, None), P(FSDP, None)),
        check_vma=False,
    )
```

```python
import functools

import jax
import jax.numpy as jnp
from jax import lax
from jax.experimental import pallas as pl
from jax.experimental.pallas import tpu as pltpu
from jax.sharding import Mesh
from jax.sharding import PartitionSpec as P

HEADS = 32
KV_HEADS = 4
HEAD = 128
QB = 128
SPAN = 1024
AXES = ("x", "yh", "core", "zh", "zl", "yl")
SIZES = (4, 2, 2, 4, 2, 2)
FSDP = ("zh", "zl", "yl")
GROUP = ("zl", "yl")
PLANE = ("x", "yh")
MEMBERS = 4

FACTOR = 1.0 / float(HEAD) ** 0.5
LOG2E = 1.4426950408889634
NEG = -1e30
F32 = jnp.float32
BF16 = jnp.bfloat16


def nt(a, b):
    return lax.dot_general(a, b, (((1,), (1,)), ((), ())), preferred_element_type=F32)


def nn(a, b):
    return lax.dot_general(a, b, (((1,), (0,)), ((), ())), preferred_element_type=F32)


def tn(a, b):
    return lax.dot_general(a, b, (((0,), (0,)), ((), ())), preferred_element_type=F32)


def shifted(block, axes, distance):
    devices = range(lax.axis_size(axes))
    route = [(i - distance, i) for i in devices if i - distance in devices]
    return lax.ppermute(block, axes, route)


def swapped(block, axes, mask):
    return lax.ppermute(block, axes, [(i, i ^ mask) for i in range(lax.axis_size(axes))])


def fanned(block):
    return [block] + [swapped(block, GROUP, k) for k in range(1, MEMBERS)]


def dealt(blocks):
    return [blocks[0]] + [swapped(blocks[k], GROUP, k) for k in range(1, MEMBERS)]


def exchange(blocks, axes):
    return lax.all_to_all(blocks, axes, split_axis=0, concat_axis=0, tiled=True)


def small(name, grid, in_specs, out_specs, out_shape, kernel, prefetch=0):
    return pl.pallas_call(
        kernel,
        grid_spec=pltpu.PrefetchScalarGridSpec(
            num_scalar_prefetch=prefetch, grid=grid, in_specs=in_specs, out_specs=out_specs
        ),
        out_shape=out_shape,
        compiler_params=pltpu.CompilerParams(vmem_limit_bytes=16 << 20),
        cost_estimate=pl.CostEstimate(flops=0, bytes_accessed=4 << 20, transcendentals=0),
        name=name,
    )


def dequantize_kernel(part_ref, b_ref, s_ref, o_ref):
    del part_ref
    for j in range(b_ref.shape[1] // QB):
        to = (j % KV_HEADS) * 2 + j // KV_HEADS
        block = b_ref[:, j * QB : (j + 1) * QB].astype(F32) * s_ref[0, :, j : j + 1]
        o_ref[:, to * QB : (to + 1) * QB] = block.astype(BF16)


def dequantize(part, blocks, scale, rows):
    cols = blocks.shape[1]
    scale = scale.reshape(scale.shape[0], 1, scale.shape[1])
    return small(
        "dequantize",
        (1,),
        [
            pl.BlockSpec((rows, cols), lambda i, p: (p[0], 0)),
            pl.BlockSpec((1,) + scale.shape[1:], lambda i, p: (p[0] * rows // QB, 0, 0)),
        ],
        pl.BlockSpec((rows, cols), lambda i, p: (0, 0)),
        jax.ShapeDtypeStruct((rows, cols), BF16),
        dequantize_kernel,
        1,
    )(part, blocks, scale)


def pack_hidden_kernel(*refs):
    o_ref = refs[-1]
    zhs = len(refs) - 1
    half = refs[0].shape[1] // 2
    for zh, ref in enumerate(refs[:-1]):
        for core in range(2):
            at = (core * zhs + zh) * half
            o_ref[0, :, at : at + half] = ref[:, core * half : (core + 1) * half]


def pack_hidden(hidden, zhs):
    tok, depth = hidden.shape
    quarter = depth // MEMBERS
    piece = quarter // zhs
    return small(
        "pack_hidden",
        (MEMBERS,),
        [pl.BlockSpec((tok, piece), lambda m, z=z: (0, z * MEMBERS + m)) for z in range(zhs)],
        pl.BlockSpec((1, tok, quarter), lambda m: (m, 0, 0)),
        jax.ShapeDtypeStruct((MEMBERS, tok, quarter), hidden.dtype),
        pack_hidden_kernel,
    )(*[hidden] * zhs)


def unpack_hidden_kernel(member_ref, *refs):
    o_ref = refs[-1]
    half = refs[0].shape[1]
    for k in range(MEMBERS):
        for core in range(2):
            at = (2 * (member_ref[0] ^ k) + core) * half
            o_ref[:, pl.ds(pl.multiple_of(at, half), half)] = refs[2 * k + core][...]


def unpack_hidden(member, pieces, zhs):
    tok, quarter = pieces[0].shape
    half = quarter // (2 * zhs)
    specs = [pl.BlockSpec((tok, half), lambda z, m, c=c: (0, c * zhs + z)) for c in range(2)]
    return small(
        "unpack_hidden",
        (zhs,),
        specs * MEMBERS,
        pl.BlockSpec((tok, 2 * half * MEMBERS), lambda z, m: (0, z)),
        jax.ShapeDtypeStruct((tok, quarter * MEMBERS), pieces[0].dtype),
        unpack_hidden_kernel,
        1,
    )(member, *[p for p in pieces for _ in range(2)])


def pack_heads_kernel(q_ref, g_ref, o_ref):
    o_ref[0, 0] = q_ref[...]
    o_ref[0, 1] = g_ref[...]


def pack_heads(queries, grad_out):
    tok, cols = queries.shape
    width = cols // MEMBERS
    block = pl.BlockSpec((tok, width), lambda m: (0, m))
    return small(
        "pack_heads",
        (MEMBERS,),
        [block, block],
        pl.BlockSpec((1, 2, tok, width), lambda m: (m, 0, 0, 0)),
        jax.ShapeDtypeStruct((MEMBERS, 2, tok, width), queries.dtype),
        pack_heads_kernel,
    )(queries, grad_out)


def unpack_heads_kernel(member_ref, *refs):
    a_ref, b_ref = refs[-2:]
    width = refs[0].shape[2]
    for k in range(MEMBERS):
        at = pl.ds(pl.multiple_of((member_ref[0] ^ k) * width, width), width)
        a_ref[:, at] = refs[k][0]
        b_ref[:, at] = refs[k][1]


def unpack_heads(member, pieces):
    _, tok, width = pieces[0].shape
    steps = 4
    rows = tok // steps
    block = pl.BlockSpec((rows, width * MEMBERS), lambda i, m: (i, 0))
    shape = jax.ShapeDtypeStruct((tok, width * MEMBERS), pieces[0].dtype)
    return small(
        "unpack_heads",
        (steps,),
        [pl.BlockSpec((2, rows, width), lambda i, m: (0, i, 0))] * MEMBERS,
        [block, block],
        [shape, shape],
        unpack_heads_kernel,
        1,
    )(member, *pieces)


def turn_kernel(x_ref, o_ref):
    o_ref[...] = x_ref[...].T


def turn(x):
    rows, cols = x.shape
    step = cols // 4
    return small(
        "turn",
        (4,),
        [pl.BlockSpec((rows, step), lambda i: (0, i))],
        pl.BlockSpec((step, rows), lambda i: (i, 0)),
        jax.ShapeDtypeStruct((cols, rows), x.dtype),
        turn_kernel,
    )(x)


def in_feature_order(w):
    xs, cores, zhs = w.shape[:3]
    return [[jnp.concatenate([w[x, c, z] for x in range(xs)], axis=0) for z in range(zhs)] for c in range(cores)]


def project_kernel(h_ref, w_ref, o_ref):
    rows = [block for line in in_feature_order(w_ref) for block in line]
    o_ref[0] = nn(h_ref[...], jnp.concatenate(rows, axis=0))


def project(hidden, weights):
    rows, depth = hidden.shape
    width = weights.shape[-1] // MEMBERS
    return pl.pallas_call(
        project_kernel,
        grid=(MEMBERS,),
        in_specs=[
            pl.BlockSpec((rows, depth), lambda h: (0, 0)),
            pl.BlockSpec(weights.shape[:-1] + (width,), lambda h: (0, 0, 0, 0, h)),
        ],
        out_specs=pl.BlockSpec((1, rows, width), lambda h: (h, 0, 0)),
        out_shape=jax.ShapeDtypeStruct((MEMBERS, rows, width), F32),
        compiler_params=pltpu.CompilerParams(vmem_limit_bytes=48 << 20),
        cost_estimate=pl.CostEstimate(
            flops=2 * rows * depth * width * MEMBERS, bytes_accessed=8 << 20, transcendentals=0
        ),
        name="project",
    )(hidden, weights)


def attention_kernel(place_ref, q_ref, g_ref, far_ref, near_ref, own_ref, *refs, steps, last):
    if last:
        before_ref, refs = refs[0], refs[1:]
        outs, (dfar_ref, dnear_ref, down_ref, kv, both, acc) = refs[:steps], refs[steps:]
    else:
        outs, (acc, kv, both) = refs[:steps], refs[steps:]
    i = pl.program_id(0)
    group = own_ref.shape[0]
    tok = q_ref.shape[2]
    pairs = q_ref.shape[3] // (2 * HEAD)
    width = SPAN + tok

    @pl.when(i == 0)
    def _():
        kv[0:group] = far_ref[...]
        kv[group : 2 * group] = near_ref[...]
        kv[2 * group :] = own_ref[...]
        acc[...] = before_ref[...] if last else jnp.zeros_like(acc)

    start = pl.multiple_of(place_ref[i] * tok, tok)
    lim = place_ref[steps + i]

    def run(masked):
        keys = kv[pl.ds(start, width), 0:HEAD]
        vals = kv[pl.ds(start, width), HEAD : 2 * HEAD]
        row = lax.broadcasted_iota(jnp.int32, (tok, 2 * tok), 0)
        col = lax.broadcasted_iota(jnp.int32, (tok, 2 * tok), 1) & (tok - 1)
        for pair in range(pairs):
            a = slice(2 * pair * HEAD, (2 * pair + 1) * HEAD)
            b = slice((2 * pair + 1) * HEAD, (2 * pair + 2) * HEAD)
            q2 = jnp.concatenate([q_ref[0, 0, :, a], q_ref[0, 0, :, b]], axis=0)
            g2 = jnp.concatenate([g_ref[0, 0, :, a], g_ref[0, 0, :, b]], axis=0)
            s = nt(keys, q2)
            s = jnp.concatenate(
                [
                    jnp.where(row > col, s[:tok], NEG),
                    s[tok:SPAN],
                    jnp.where(row <= col, s[SPAN:], NEG),
                ],
                axis=0,
            )
            if masked:
                s = jnp.where(lax.broadcasted_iota(jnp.int32, s.shape, 0) >= lim, s, NEG)
            top = jnp.max(s, axis=0, keepdims=True) * (FACTOR * LOG2E)
            expd = jnp.exp2(s * (FACTOR * LOG2E) - top)
            probs = expd * (1.0 / jnp.sum(expd, axis=0, keepdims=True))
            probs_b = probs.astype(BF16)
            dprobs = nt(vals, g2)
            delta = jnp.sum(probs * dprobs, axis=0, keepdims=True)
            dscores = (probs * (dprobs - delta) * FACTOR).astype(BF16)
            acc[pl.ds(start, width), 0:HEAD] += nn(dscores, q2)
            acc[pl.ds(start, width), HEAD : 2 * HEAD] += nn(probs_b, g2)
            output = tn(probs_b, vals).astype(BF16)
            gradq = tn(dscores, keys).astype(BF16)
            both[0, :, a] = output[:tok]
            both[0, :, b] = output[tok:]
            both[1, :, a] = gradq[:tok]
            both[1, :, b] = gradq[tok:]

    @pl.when(lim <= 0)
    def _():
        run(False)

    @pl.when(lim > 0)
    def _():
        run(True)

    for step, out_ref in enumerate(outs):

        @pl.when(i == step)
        def _(out_ref=out_ref):
            out_ref[...] = both[...]

    if last:

        @pl.when(i == steps - 1)
        def _():
            dfar_ref[...] = acc[0:group].astype(dfar_ref.dtype)
            dnear_ref[...] = acc[group : 2 * group].astype(dnear_ref.dtype)
            down_ref[...] = acc[2 * group :]


def attention(place, queries, far, near, own, before=None):
    steps = place.shape[0] // 2
    last = before is not None
    tok, cols = queries.shape[2:]
    group, both = own.shape
    whole = pl.BlockSpec((group, both), lambda i, p: (0, 0))
    window = pl.BlockSpec((3 * group, both), lambda i, p: (0, 0))
    out = (2, tok, cols)
    part = jax.ShapeDtypeStruct(own.shape, BF16)
    scratch = [pltpu.VMEM((3 * group, both), BF16), pltpu.VMEM(out, BF16)]
    if last:
        scratch.append(pltpu.VMEM((3 * group, both), F32))
    return pl.pallas_call(
        functools.partial(attention_kernel, steps=steps, last=last),
        grid_spec=pltpu.PrefetchScalarGridSpec(
            num_scalar_prefetch=1,
            grid=(steps,),
            in_specs=[
                pl.BlockSpec((1, 1, tok, cols), lambda i, p: (p[i], 0, 0, 0)),
                pl.BlockSpec((1, 1, tok, cols), lambda i, p: (p[i], 1, 0, 0)),
                whole,
                whole,
                whole,
            ]
            + ([window] if last else []),
            out_specs=[pl.BlockSpec(out, lambda i, p: (0, 0, 0))] * steps
            + ([whole] * 3 if last else [window]),
            scratch_shapes=scratch,
        ),
        out_shape=[jax.ShapeDtypeStruct(out, BF16)] * steps
        + (
            [part, part, jax.ShapeDtypeStruct(own.shape, F32)]
            if last
            else [jax.ShapeDtypeStruct((3 * group, both), F32)]
        ),
        compiler_params=pltpu.CompilerParams(vmem_limit_bytes=48 << 20),
        cost_estimate=pl.CostEstimate(
            flops=15_000_000_000, bytes_accessed=4 << 20, transcendentals=2_500_000
        ),
        name="attention",
    )(*([place, queries, queries, far, near, own] + ([before] if last else [])))


def grad_hidden_kernel(member_ref, d0, d1, d2, d3, w_ref, o_ref, rows):
    rows[...] = in_feature_order(w_ref)[0][0]
    total = None
    for k, d in enumerate((d0, d1, d2, d3)):
        width = d.shape[1]
        at = pl.multiple_of((member_ref[0] ^ k) * width, width)
        term = nt(d[...], rows[:, pl.ds(at, width)])
        total = term if total is None else total + term
    tok = o_ref.shape[1]
    for t in range(MEMBERS):
        o_ref[member_ref[0] ^ t] = total[t * tok : (t + 1) * tok].astype(BF16)


def grad_hidden_quarter(member, pieces, weights):
    rows, width = pieces[0].shape
    xs, cores, zhs, part, cols = weights.shape
    step = xs * part
    depth = step * cores * zhs
    piece = pl.BlockSpec((rows, width), lambda i, m: (0, 0))
    return pl.pallas_call(
        grad_hidden_kernel,
        grid_spec=pltpu.PrefetchScalarGridSpec(
            num_scalar_prefetch=1,
            grid=(depth // step,),
            in_specs=[piece] * 4
            + [pl.BlockSpec((xs, 1, 1, part, cols), lambda i, m: (0, i // zhs, i % zhs, 0, 0))],
            scratch_shapes=[pltpu.VMEM((step, cols), BF16)],
            out_specs=pl.BlockSpec((MEMBERS, rows // MEMBERS, step), lambda i, m: (0, 0, i)),
        ),
        out_shape=jax.ShapeDtypeStruct((MEMBERS, rows // MEMBERS, depth), BF16),
        compiler_params=pltpu.CompilerParams(vmem_limit_bytes=32 << 20),
        cost_estimate=pl.CostEstimate(
            flops=2 * rows * depth * cols, bytes_accessed=8 << 20, transcendentals=0
        ),
        name="grad_hidden",
    )(member, *pieces, weights)


def weight_grad_kernel(place_ref, h_ref, d0, d1, d2, d3, o_ref):
    xs, yhs, _, rows, cols = o_ref.shape
    for k, d in enumerate((d0, d1, d2, d3)):
        at = pl.multiple_of((place_ref[0] ^ k) * HEAD, HEAD)
        term = nn(h_ref[...], d[...]).astype(o_ref.dtype).reshape(xs, yhs, rows, 2 * HEAD)
        o_ref[:, :, 0, :, pl.ds(at, HEAD)] = term[..., :HEAD]
        o_ref[:, :, 0, :, pl.ds(cols // 2 + at, HEAD)] = term[..., HEAD:]


def weight_grad_share(place, turned, pieces, steps, dtype):
    feats, tokens = turned.shape
    both = pieces[0].shape[1]
    cols = both * KV_HEADS
    step = feats // (2 * steps)
    xs, yhs = lax.axis_size("x"), lax.axis_size("yh")
    out = (xs, yhs, steps, step // (xs * yhs), cols)
    return pl.pallas_call(
        weight_grad_kernel,
        grid_spec=pltpu.PrefetchScalarGridSpec(
            num_scalar_prefetch=1,
            grid=(steps,),
            in_specs=[pl.BlockSpec((step, tokens), lambda i, p: (p[1] * steps + i, 0))]
            + [pl.BlockSpec((tokens, both), lambda i, p: (0, 0))] * 4,
            out_specs=pl.BlockSpec((xs, yhs, 1) + out[3:], lambda i, p: (0, 0, i, 0, 0)),
        ),
        out_shape=jax.ShapeDtypeStruct(out, dtype),
        compiler_params=pltpu.CompilerParams(vmem_limit_bytes=32 << 20),
        cost_estimate=pl.CostEstimate(
            flops=feats * tokens * cols, bytes_accessed=5 << 20, transcendentals=0
        ),
        name="weight_grad",
    )(place, turned, *pieces)


def merge_kernel(core_ref, mine_ref, theirs_ref, o_ref):
    @pl.when(pl.program_id(0) == core_ref[0])
    def _():
        o_ref[...] = mine_ref[...].astype(F32)

    @pl.when(pl.program_id(0) != core_ref[0])
    def _():
        o_ref[...] = theirs_ref[...].astype(F32)


def merge(core, mine, theirs):
    rows, cols = mine.shape
    block = pl.BlockSpec((rows, cols), lambda i, c: (0, 0))
    return small(
        "merge",
        (2,),
        [block, block],
        pl.BlockSpec((rows, cols), lambda i, c: (i, 0)),
        jax.ShapeDtypeStruct((2 * rows, cols), F32),
        merge_kernel,
        1,
    )(core, mine, theirs)


def body(hidden, kv_blocks, kv_scale, queries, grad_out):
    tok = hidden.shape[0]
    shard, kv_cols = kv_blocks.shape
    half = shard // 2
    zh = lax.axis_index("zh")
    core = lax.axis_index("core").reshape(1)
    member = lax.axis_index(GROUP).reshape(1)
    xs, zhs = lax.axis_size("x"), lax.axis_size("zh")

    part = core * xs + lax.axis_index("x")
    rows = dequantize(part, kv_blocks, kv_scale, half // xs)
    weights = lax.all_gather(rows, ("x", "core", "zh"), axis=0, tiled=True)
    weights = weights.reshape(xs, 2, zhs, half // xs, kv_cols)
    quarter = exchange(pack_hidden(hidden, zhs), GROUP).reshape(MEMBERS * tok, -1)
    heads = exchange(pack_heads(queries, grad_out), GROUP)

    weights, quarter, heads = lax.optimization_barrier((weights, quarter, heads))
    partial = exchange(project(quarter, weights), GROUP)
    own = jnp.sum(partial, axis=0).astype(BF16)
    far = shifted(own, AXES, 2 * MEMBERS)
    near = shifted(own, AXES, MEMBERS)
    quarter, own = lax.optimization_barrier((quarter, own))
    turned = turn(quarter)
    far, near, turned = lax.optimization_barrier((far, near, turned))

    first = lax.axis_index(AXES) // MEMBERS * MEMBERS
    order = member ^ jnp.array([1, 2, 3, 0], jnp.int32)
    lim = jnp.maximum(0, SPAN - (first + order) * tok)
    out1, out2, before = attention(
        jnp.concatenate([order[:2], lim[:2]]).astype(jnp.int32), heads, far, near, own
    )
    outs = [swapped(out1, GROUP, 1), swapped(out2, GROUP, 2)]
    out3, out0, dfar, dnear, down = attention(
        jnp.concatenate([order[2:], lim[2:]]).astype(jnp.int32), heads, far, near, own, before
    )
    dfar, dnear, outs = lax.optimization_barrier((dfar, dnear, outs))
    from_far = shifted(dfar, AXES, -2 * MEMBERS).astype(F32)
    from_near = shifted(dnear, AXES, -MEMBERS).astype(F32)
    all_grad = (down + from_near + from_far).astype(BF16)
    inside = down + jnp.where(zh + 1 < zhs, from_near, 0.0) + jnp.where(zh + 2 < zhs, from_far, 0.0)
    seg_grad = inside.astype(BF16)

    alls = fanned(all_grad)
    theirs = weight_grad_share(jnp.concatenate([member, 1 - core]), turned, alls, zhs, BF16)
    mine = weight_grad_share(jnp.concatenate([member, core]), turned, alls, zhs, F32)

    seg_grad, out3, theirs = lax.optimization_barrier((seg_grad, out3, theirs))
    segs = fanned(seg_grad)
    mine = (mine + swapped(theirs, "core", 1).astype(F32)).astype(BF16)
    mine, segs = lax.optimization_barrier((mine, segs))
    back = grad_hidden_quarter(member, segs, weights)
    outs = [out0] + outs + [swapped(out3, GROUP, 3)]
    parts = exchange(mine, "x")
    parts, outs, back = lax.optimization_barrier((parts, outs, back))
    backs = dealt(back)
    parts = jnp.sum(parts.astype(F32), axis=0).astype(BF16)
    parts = exchange(parts.reshape((-1,) + parts.shape[2:]), ("yh", "zh"))
    summed = jnp.sum(parts.astype(F32), axis=0).astype(BF16)
    backs, summed = lax.optimization_barrier((backs, summed))
    spread = jnp.broadcast_to(summed[None], (half // summed.shape[0],) + summed.shape)
    spread = exchange(spread, PLANE).reshape(half, kv_cols)
    weight_grad = merge(core, spread, swapped(spread, "core", 1))
    attn_out, grad_queries = unpack_heads(member, outs)
    grad_hidden = unpack_hidden(member, backs, zhs)
    return (attn_out, grad_queries, grad_hidden, weight_grad)


def solution(mesh):
    finer = Mesh(mesh.devices.reshape(SIZES), AXES)
    placed = (P(AXES, None), P(FSDP, None), P(FSDP, None), P(AXES, None), P(AXES, None))
    return jax.shard_map(
        body,
        mesh=finer,
        in_specs=placed,
        out_specs=(P(AXES, None), P(AXES, None), P(AXES, None), P(FSDP, None)),
        check_vma=False,
    )
```

```python
import functools

import jax
import jax.numpy as jnp
from jax import lax
from jax.experimental import pallas as pl
from jax.experimental.pallas import tpu as pltpu
from jax.sharding import Mesh
from jax.sharding import PartitionSpec as P

HEADS = 32
KV_HEADS = 4
HEAD = 128
QB = 128
SPAN = 1024
AXES = ("x", "yh", "core", "zh", "zl", "yl")
SIZES = (4, 2, 2, 4, 2, 2)
FSDP = ("zh", "zl", "yl")
GROUP = ("zl", "yl")
PLANE = ("x", "yh")
MEMBERS = 4

FACTOR = 1.0 / float(HEAD) ** 0.5
LOG2E = 1.4426950408889634
NEG = -1e30
F32 = jnp.float32
BF16 = jnp.bfloat16


def nt(a, b):
    return lax.dot_general(a, b, (((1,), (1,)), ((), ())), preferred_element_type=F32)


def nn(a, b):
    return lax.dot_general(a, b, (((1,), (0,)), ((), ())), preferred_element_type=F32)


def tn(a, b):
    return lax.dot_general(a, b, (((0,), (0,)), ((), ())), preferred_element_type=F32)


def shifted(block, axes, distance):
    devices = range(lax.axis_size(axes))
    route = [(i - distance, i) for i in devices if i - distance in devices]
    return lax.ppermute(block, axes, route)


def swapped(block, axes, mask):
    return lax.ppermute(block, axes, [(i, i ^ mask) for i in range(lax.axis_size(axes))])


def fanned(block):
    return [block] + [swapped(block, GROUP, k) for k in range(1, MEMBERS)]


def dealt(blocks):
    return [blocks[0]] + [swapped(blocks[k], GROUP, k) for k in range(1, MEMBERS)]


def exchange(blocks, axes):
    return lax.all_to_all(blocks, axes, split_axis=0, concat_axis=0, tiled=True)


def small(name, grid, in_specs, out_specs, out_shape, kernel, prefetch=0):
    return pl.pallas_call(
        kernel,
        grid_spec=pltpu.PrefetchScalarGridSpec(
            num_scalar_prefetch=prefetch, grid=grid, in_specs=in_specs, out_specs=out_specs
        ),
        out_shape=out_shape,
        compiler_params=pltpu.CompilerParams(vmem_limit_bytes=16 << 20),
        cost_estimate=pl.CostEstimate(flops=0, bytes_accessed=4 << 20, transcendentals=0),
        name=name,
    )


def dequantize_kernel(part_ref, b_ref, s_ref, o_ref):
    del part_ref
    for j in range(b_ref.shape[1] // QB):
        to = (j % KV_HEADS) * 2 + j // KV_HEADS
        block = b_ref[:, j * QB : (j + 1) * QB].astype(F32) * s_ref[0, :, j : j + 1]
        o_ref[:, to * QB : (to + 1) * QB] = block.astype(BF16)


def dequantize(part, blocks, scale, rows):
    cols = blocks.shape[1]
    scale = scale.reshape(scale.shape[0], 1, scale.shape[1])
    return small(
        "dequantize",
        (1,),
        [
            pl.BlockSpec((rows, cols), lambda i, p: (p[0], 0)),
            pl.BlockSpec((1,) + scale.shape[1:], lambda i, p: (p[0] * rows // QB, 0, 0)),
        ],
        pl.BlockSpec((rows, cols), lambda i, p: (0, 0)),
        jax.ShapeDtypeStruct((rows, cols), BF16),
        dequantize_kernel,
        1,
    )(part, blocks, scale)


def pack_hidden_kernel(*refs):
    o_ref = refs[-1]
    zhs = len(refs) - 1
    half = refs[0].shape[1] // 2
    for zh, ref in enumerate(refs[:-1]):
        for core in range(2):
            at = (core * zhs + zh) * half
            o_ref[0, :, at : at + half] = ref[:, core * half : (core + 1) * half]


def pack_hidden(hidden, zhs):
    tok, depth = hidden.shape
    quarter = depth // MEMBERS
    piece = quarter // zhs
    return small(
        "pack_hidden",
        (MEMBERS,),
        [pl.BlockSpec((tok, piece), lambda m, z=z: (0, z * MEMBERS + m)) for z in range(zhs)],
        pl.BlockSpec((1, tok, quarter), lambda m: (m, 0, 0)),
        jax.ShapeDtypeStruct((MEMBERS, tok, quarter), hidden.dtype),
        pack_hidden_kernel,
    )(*[hidden] * zhs)


def unpack_hidden_kernel(member_ref, *refs):
    o_ref = refs[-1]
    half = refs[0].shape[1]
    for k in range(MEMBERS):
        for core in range(2):
            at = (2 * (member_ref[0] ^ k) + core) * half
            o_ref[:, pl.ds(pl.multiple_of(at, half), half)] = refs[2 * k + core][...]


def unpack_hidden(member, pieces, zhs):
    tok, quarter = pieces[0].shape
    half = quarter // (2 * zhs)
    specs = [pl.BlockSpec((tok, half), lambda z, m, c=c: (0, c * zhs + z)) for c in range(2)]
    return small(
        "unpack_hidden",
        (zhs,),
        specs * MEMBERS,
        pl.BlockSpec((tok, 2 * half * MEMBERS), lambda z, m: (0, z)),
        jax.ShapeDtypeStruct((tok, quarter * MEMBERS), pieces[0].dtype),
        unpack_hidden_kernel,
        1,
    )(member, *[p for p in pieces for _ in range(2)])


def pack_heads_kernel(q_ref, g_ref, o_ref):
    o_ref[0, 0] = q_ref[...]
    o_ref[0, 1] = g_ref[...]


def pack_heads(queries, grad_out):
    tok, cols = queries.shape
    width = cols // MEMBERS
    block = pl.BlockSpec((tok, width), lambda m: (0, m))
    return small(
        "pack_heads",
        (MEMBERS,),
        [block, block],
        pl.BlockSpec((1, 2, tok, width), lambda m: (m, 0, 0, 0)),
        jax.ShapeDtypeStruct((MEMBERS, 2, tok, width), queries.dtype),
        pack_heads_kernel,
    )(queries, grad_out)


def unpack_heads_kernel(member_ref, *refs):
    a_ref, b_ref = refs[-2:]
    width = refs[0].shape[2]
    for k in range(MEMBERS):
        at = pl.ds(pl.multiple_of((member_ref[0] ^ k) * width, width), width)
        a_ref[:, at] = refs[k][0]
        b_ref[:, at] = refs[k][1]


def unpack_heads(member, pieces):
    _, tok, width = pieces[0].shape
    steps = 4
    rows = tok // steps
    block = pl.BlockSpec((rows, width * MEMBERS), lambda i, m: (i, 0))
    shape = jax.ShapeDtypeStruct((tok, width * MEMBERS), pieces[0].dtype)
    return small(
        "unpack_heads",
        (steps,),
        [pl.BlockSpec((2, rows, width), lambda i, m: (0, i, 0))] * MEMBERS,
        [block, block],
        [shape, shape],
        unpack_heads_kernel,
        1,
    )(member, *pieces)


def turn_kernel(x_ref, o_ref):
    o_ref[...] = x_ref[...].T


def turn(x):
    rows, cols = x.shape
    step = cols // 4
    return small(
        "turn",
        (4,),
        [pl.BlockSpec((rows, step), lambda i: (0, i))],
        pl.BlockSpec((step, rows), lambda i: (i, 0)),
        jax.ShapeDtypeStruct((cols, rows), x.dtype),
        turn_kernel,
    )(x)


def in_feature_order(w):
    xs, cores, zhs = w.shape[:3]
    return [[jnp.concatenate([w[x, c, z] for x in range(xs)], axis=0) for z in range(zhs)] for c in range(cores)]


def project_kernel(h_ref, w_ref, o_ref):
    rows = [block for line in in_feature_order(w_ref) for block in line]
    o_ref[0] = nn(h_ref[...], jnp.concatenate(rows, axis=0))


def project(hidden, weights):
    rows, depth = hidden.shape
    width = weights.shape[-1] // MEMBERS
    return pl.pallas_call(
        project_kernel,
        grid=(MEMBERS,),
        in_specs=[
            pl.BlockSpec((rows, depth), lambda h: (0, 0)),
            pl.BlockSpec(weights.shape[:-1] + (width,), lambda h: (0, 0, 0, 0, h)),
        ],
        out_specs=pl.BlockSpec((1, rows, width), lambda h: (h, 0, 0)),
        out_shape=jax.ShapeDtypeStruct((MEMBERS, rows, width), F32),
        compiler_params=pltpu.CompilerParams(vmem_limit_bytes=20 << 20),
        cost_estimate=pl.CostEstimate(
            flops=2 * rows * depth * width * MEMBERS, bytes_accessed=8 << 20, transcendentals=0
        ),
        name="project",
    )(hidden, weights)


def attention_kernel(place_ref, q_ref, g_ref, far_ref, near_ref, own_ref, *refs, steps, last):
    if last:
        before_ref, refs = refs[0], refs[1:]
        outs, (dfar_ref, dnear_ref, down_ref, kv, both, acc) = refs[:steps], refs[steps:]
    else:
        outs, (acc, kv, both) = refs[:steps], refs[steps:]
    i = pl.program_id(0)
    group = own_ref.shape[0]
    tok = q_ref.shape[2]
    pairs = q_ref.shape[3] // (2 * HEAD)
    width = SPAN + tok

    @pl.when(i == 0)
    def _():
        kv[0:group] = far_ref[...]
        kv[group : 2 * group] = near_ref[...]
        kv[2 * group :] = own_ref[...]
        acc[...] = before_ref[...] if last else jnp.zeros_like(acc)

    start = pl.multiple_of(place_ref[i] * tok, tok)
    lim = place_ref[steps + i]

    def run(masked):
        keys = kv[pl.ds(start, width), 0:HEAD]
        vals = kv[pl.ds(start, width), HEAD : 2 * HEAD]
        row = lax.broadcasted_iota(jnp.int32, (tok, 2 * tok), 0)
        col = lax.broadcasted_iota(jnp.int32, (tok, 2 * tok), 1) & (tok - 1)
        for pair in range(pairs):
            a = slice(2 * pair * HEAD, (2 * pair + 1) * HEAD)
            b = slice((2 * pair + 1) * HEAD, (2 * pair + 2) * HEAD)
            q2 = jnp.concatenate([q_ref[0, 0, :, a], q_ref[0, 0, :, b]], axis=0)
            g2 = jnp.concatenate([g_ref[0, 0, :, a], g_ref[0, 0, :, b]], axis=0)
            s = nt(keys, q2)
            s = jnp.concatenate(
                [
                    jnp.where(row > col, s[:tok], NEG),
                    s[tok:SPAN],
                    jnp.where(row <= col, s[SPAN:], NEG),
                ],
                axis=0,
            )
            if masked:
                s = jnp.where(lax.broadcasted_iota(jnp.int32, s.shape, 0) >= lim, s, NEG)
            top = jnp.max(s, axis=0, keepdims=True) * (FACTOR * LOG2E)
            expd = jnp.exp2(s * (FACTOR * LOG2E) - top)
            probs = expd * (1.0 / jnp.sum(expd, axis=0, keepdims=True))
            probs_b = probs.astype(BF16)
            dprobs = nt(vals, g2)
            delta = jnp.sum(probs * dprobs, axis=0, keepdims=True)
            dscores = (probs * (dprobs - delta) * FACTOR).astype(BF16)
            acc[pl.ds(start, width), 0:HEAD] += nn(dscores, q2)
            acc[pl.ds(start, width), HEAD : 2 * HEAD] += nn(probs_b, g2)
            output = tn(probs_b, vals).astype(BF16)
            gradq = tn(dscores, keys).astype(BF16)
            both[0, :, a] = output[:tok]
            both[0, :, b] = output[tok:]
            both[1, :, a] = gradq[:tok]
            both[1, :, b] = gradq[tok:]

    @pl.when(lim <= 0)
    def _():
        run(False)

    @pl.when(lim > 0)
    def _():
        run(True)

    for step, out_ref in enumerate(outs):

        @pl.when(i == step)
        def _(out_ref=out_ref):
            out_ref[...] = both[...]

    if last:

        @pl.when(i == steps - 1)
        def _():
            dfar_ref[...] = acc[0:group].astype(dfar_ref.dtype)
            dnear_ref[...] = acc[group : 2 * group].astype(dnear_ref.dtype)
            down_ref[...] = acc[2 * group :]


def attention(place, queries, far, near, own, before=None):
    steps = place.shape[0] // 2
    last = before is not None
    tok, cols = queries.shape[2:]
    group, both = own.shape
    whole = pl.BlockSpec((group, both), lambda i, p: (0, 0))
    window = pl.BlockSpec((3 * group, both), lambda i, p: (0, 0))
    out = (2, tok, cols)
    part = jax.ShapeDtypeStruct(own.shape, BF16)
    scratch = [pltpu.VMEM((3 * group, both), BF16), pltpu.VMEM(out, BF16)]
    if last:
        scratch.append(pltpu.VMEM((3 * group, both), F32))
    return pl.pallas_call(
        functools.partial(attention_kernel, steps=steps, last=last),
        grid_spec=pltpu.PrefetchScalarGridSpec(
            num_scalar_prefetch=1,
            grid=(steps,),
            in_specs=[
                pl.BlockSpec((1, 1, tok, cols), lambda i, p: (p[i], 0, 0, 0)),
                pl.BlockSpec((1, 1, tok, cols), lambda i, p: (p[i], 1, 0, 0)),
                whole,
                whole,
                whole,
            ]
            + ([window] if last else []),
            out_specs=[pl.BlockSpec(out, lambda i, p: (0, 0, 0))] * steps
            + ([whole] * 3 if last else [window]),
            scratch_shapes=scratch,
        ),
        out_shape=[jax.ShapeDtypeStruct(out, BF16)] * steps
        + (
            [part, part, jax.ShapeDtypeStruct(own.shape, F32)]
            if last
            else [jax.ShapeDtypeStruct((3 * group, both), F32)]
        ),
        compiler_params=pltpu.CompilerParams(vmem_limit_bytes=20 << 20),
        cost_estimate=pl.CostEstimate(
            flops=15_000_000_000, bytes_accessed=4 << 20, transcendentals=2_500_000
        ),
        name="attention",
    )(*([place, queries, queries, far, near, own] + ([before] if last else [])))


def grad_hidden_kernel(member_ref, d0, d1, d2, d3, w_ref, o_ref, rows):
    rows[...] = in_feature_order(w_ref)[0][0]
    total = None
    for k, d in enumerate((d0, d1, d2, d3)):
        width = d.shape[1]
        at = pl.multiple_of((member_ref[0] ^ k) * width, width)
        term = nt(d[...], rows[:, pl.ds(at, width)])
        total = term if total is None else total + term
    tok = o_ref.shape[1]
    for t in range(MEMBERS):
        o_ref[member_ref[0] ^ t] = total[t * tok : (t + 1) * tok].astype(BF16)


def grad_hidden_quarter(member, pieces, weights):
    rows, width = pieces[0].shape
    xs, cores, zhs, part, cols = weights.shape
    step = xs * part
    depth = step * cores * zhs
    piece = pl.BlockSpec((rows, width), lambda i, m: (0, 0))
    return pl.pallas_call(
        grad_hidden_kernel,
        grid_spec=pltpu.PrefetchScalarGridSpec(
            num_scalar_prefetch=1,
            grid=(depth // step,),
            in_specs=[piece] * 4
            + [pl.BlockSpec((xs, 1, 1, part, cols), lambda i, m: (0, i // zhs, i % zhs, 0, 0))],
            scratch_shapes=[pltpu.VMEM((step, cols), BF16)],
            out_specs=pl.BlockSpec((MEMBERS, rows // MEMBERS, step), lambda i, m: (0, 0, i)),
        ),
        out_shape=jax.ShapeDtypeStruct((MEMBERS, rows // MEMBERS, depth), BF16),
        compiler_params=pltpu.CompilerParams(vmem_limit_bytes=14 << 20),
        cost_estimate=pl.CostEstimate(
            flops=2 * rows * depth * cols, bytes_accessed=8 << 20, transcendentals=0
        ),
        name="grad_hidden",
    )(member, *pieces, weights)


def weight_grad_kernel(place_ref, h_ref, d0, d1, d2, d3, o_ref):
    xs, yhs, _, rows, cols = o_ref.shape
    for k, d in enumerate((d0, d1, d2, d3)):
        at = pl.multiple_of((place_ref[0] ^ k) * HEAD, HEAD)
        term = nn(h_ref[...], d[...]).astype(o_ref.dtype).reshape(xs, yhs, rows, 2 * HEAD)
        o_ref[:, :, 0, :, pl.ds(at, HEAD)] = term[..., :HEAD]
        o_ref[:, :, 0, :, pl.ds(cols // 2 + at, HEAD)] = term[..., HEAD:]


def weight_grad_share(place, turned, pieces, steps, dtype):
    feats, tokens = turned.shape
    both = pieces[0].shape[1]
    cols = both * KV_HEADS
    step = feats // (2 * steps)
    xs, yhs = lax.axis_size("x"), lax.axis_size("yh")
    out = (xs, yhs, steps, step // (xs * yhs), cols)
    return pl.pallas_call(
        weight_grad_kernel,
        grid_spec=pltpu.PrefetchScalarGridSpec(
            num_scalar_prefetch=1,
            grid=(steps,),
            in_specs=[pl.BlockSpec((step, tokens), lambda i, p: (p[1] * steps + i, 0))]
            + [pl.BlockSpec((tokens, both), lambda i, p: (0, 0))] * 4,
            out_specs=pl.BlockSpec((xs, yhs, 1) + out[3:], lambda i, p: (0, 0, i, 0, 0)),
        ),
        out_shape=jax.ShapeDtypeStruct(out, dtype),
        compiler_params=pltpu.CompilerParams(vmem_limit_bytes=14 << 20),
        cost_estimate=pl.CostEstimate(
            flops=feats * tokens * cols, bytes_accessed=5 << 20, transcendentals=0
        ),
        name="weight_grad",
    )(place, turned, *pieces)


def merge_kernel(core_ref, mine_ref, theirs_ref, o_ref):
    @pl.when(pl.program_id(0) == core_ref[0])
    def _():
        o_ref[...] = mine_ref[...].astype(F32)

    @pl.when(pl.program_id(0) != core_ref[0])
    def _():
        o_ref[...] = theirs_ref[...].astype(F32)


def merge(core, mine, theirs):
    rows, cols = mine.shape
    block = pl.BlockSpec((rows, cols), lambda i, c: (0, 0))
    return small(
        "merge",
        (2,),
        [block, block],
        pl.BlockSpec((rows, cols), lambda i, c: (i, 0)),
        jax.ShapeDtypeStruct((2 * rows, cols), F32),
        merge_kernel,
        1,
    )(core, mine, theirs)


def body(hidden, kv_blocks, kv_scale, queries, grad_out):
    tok = hidden.shape[0]
    shard, kv_cols = kv_blocks.shape
    half = shard // 2
    zh = lax.axis_index("zh")
    core = lax.axis_index("core").reshape(1)
    member = lax.axis_index(GROUP).reshape(1)
    xs, zhs = lax.axis_size("x"), lax.axis_size("zh")

    part = core * xs + lax.axis_index("x")
    rows = dequantize(part, kv_blocks, kv_scale, half // xs)
    weights = lax.all_gather(rows, ("x", "core", "zh"), axis=0, tiled=True)
    weights = weights.reshape(xs, 2, zhs, half // xs, kv_cols)
    quarter = exchange(pack_hidden(hidden, zhs), GROUP).reshape(MEMBERS * tok, -1)
    heads = exchange(pack_heads(queries, grad_out), GROUP)

    weights, quarter, heads = lax.optimization_barrier((weights, quarter, heads))
    partial = exchange(project(quarter, weights), GROUP)
    own = jnp.sum(partial, axis=0).astype(BF16)
    far = shifted(own, AXES, 2 * MEMBERS)
    near = shifted(own, AXES, MEMBERS)
    quarter, own = lax.optimization_barrier((quarter, own))
    turned = turn(quarter)
    far, near, turned = lax.optimization_barrier((far, near, turned))

    first = lax.axis_index(AXES) // MEMBERS * MEMBERS
    order = member ^ jnp.array([1, 2, 3, 0], jnp.int32)
    lim = jnp.maximum(0, SPAN - (first + order) * tok)
    out1, out2, before = attention(
        jnp.concatenate([order[:2], lim[:2]]).astype(jnp.int32), heads, far, near, own
    )
    outs = [swapped(out1, GROUP, 1), swapped(out2, GROUP, 2)]
    out3, out0, dfar, dnear, down = attention(
        jnp.concatenate([order[2:], lim[2:]]).astype(jnp.int32), heads, far, near, own, before
    )
    dfar, dnear, outs = lax.optimization_barrier((dfar, dnear, outs))
    from_far = shifted(dfar, AXES, -2 * MEMBERS).astype(F32)
    from_near = shifted(dnear, AXES, -MEMBERS).astype(F32)
    all_grad = (down + from_near + from_far).astype(BF16)
    inside = down + jnp.where(zh + 1 < zhs, from_near, 0.0) + jnp.where(zh + 2 < zhs, from_far, 0.0)
    seg_grad = inside.astype(BF16)

    alls = fanned(all_grad)
    theirs = weight_grad_share(jnp.concatenate([member, 1 - core]), turned, alls, zhs, BF16)
    mine = weight_grad_share(jnp.concatenate([member, core]), turned, alls, zhs, F32)

    seg_grad, out3, theirs = lax.optimization_barrier((seg_grad, out3, theirs))
    segs = fanned(seg_grad)
    mine = (mine + swapped(theirs, "core", 1).astype(F32)).astype(BF16)
    mine, segs = lax.optimization_barrier((mine, segs))
    back = grad_hidden_quarter(member, segs, weights)
    outs = [out0] + outs + [swapped(out3, GROUP, 3)]
    parts = exchange(mine, "x")
    parts, outs, backs = lax.optimization_barrier((parts, outs, dealt(back)))
    parts = jnp.sum(parts.astype(F32), axis=0).astype(BF16)
    parts = exchange(parts.reshape((-1,) + parts.shape[2:]), ("yh", "zh"))
    summed = jnp.sum(parts.astype(F32), axis=0).astype(BF16)
    attn_out, grad_queries = unpack_heads(member, outs)
    attn_out, grad_queries, summed = lax.optimization_barrier((attn_out, grad_queries, summed))
    spread = jnp.broadcast_to(summed[None], (half // summed.shape[0],) + summed.shape)
    spread = exchange(spread, PLANE)
    grad_hidden = unpack_hidden(member, backs, zhs)
    grad_hidden, spread = lax.optimization_barrier((grad_hidden, spread))
    spread = spread.reshape(half, kv_cols)
    weight_grad = merge(core, spread, swapped(spread, "core", 1))
    return (attn_out, grad_queries, grad_hidden, weight_grad)


def solution(mesh):
    finer = Mesh(mesh.devices.reshape(SIZES), AXES)
    placed = (P(AXES, None), P(FSDP, None), P(FSDP, None), P(AXES, None), P(AXES, None))
    return jax.shard_map(
        body,
        mesh=finer,
        in_specs=placed,
        out_specs=(P(AXES, None), P(AXES, None), P(AXES, None), P(FSDP, None)),
        check_vma=False,
    )
```

```python
import functools

import jax
import jax.numpy as jnp
from jax import lax
from jax.experimental import pallas as pl
from jax.experimental.pallas import tpu as pltpu
from jax.sharding import Mesh
from jax.sharding import PartitionSpec as P

HEADS = 32
KV_HEADS = 4
HEAD = 128
QB = 128
SPAN = 1024
AXES = ("x", "yh", "core", "zh", "zl", "yl")
SIZES = (4, 2, 2, 4, 2, 2)
FSDP = ("zh", "zl", "yl")
GROUP = ("zl", "yl")
PLANE = ("x", "yh")
MEMBERS = 4

FACTOR = 1.0 / float(HEAD) ** 0.5
LOG2E = 1.4426950408889634
NEG = -1e30
F32 = jnp.float32
BF16 = jnp.bfloat16


def nt(a, b):
    return lax.dot_general(a, b, (((1,), (1,)), ((), ())), preferred_element_type=F32)


def nn(a, b):
    return lax.dot_general(a, b, (((1,), (0,)), ((), ())), preferred_element_type=F32)


def tn(a, b):
    return lax.dot_general(a, b, (((0,), (0,)), ((), ())), preferred_element_type=F32)


def shifted(block, axes, distance):
    devices = range(lax.axis_size(axes))
    route = [(i - distance, i) for i in devices if i - distance in devices]
    return lax.ppermute(block, axes, route)


def swapped(block, axes, mask):
    return lax.ppermute(block, axes, [(i, i ^ mask) for i in range(lax.axis_size(axes))])


def fanned(block):
    return [block] + [swapped(block, GROUP, k) for k in range(1, MEMBERS)]


def dealt(blocks):
    return [blocks[0]] + [swapped(blocks[k], GROUP, k) for k in range(1, MEMBERS)]


def exchange(blocks, axes):
    return lax.all_to_all(blocks, axes, split_axis=0, concat_axis=0, tiled=True)


def small(name, grid, in_specs, out_specs, out_shape, kernel, prefetch=0):
    return pl.pallas_call(
        kernel,
        grid_spec=pltpu.PrefetchScalarGridSpec(
            num_scalar_prefetch=prefetch, grid=grid, in_specs=in_specs, out_specs=out_specs
        ),
        out_shape=out_shape,
        compiler_params=pltpu.CompilerParams(vmem_limit_bytes=16 << 20),
        cost_estimate=pl.CostEstimate(flops=0, bytes_accessed=4 << 20, transcendentals=0),
        name=name,
    )


def dequantize_kernel(place_ref, k_ref, v_ref, s_ref, o_ref):
    del place_ref
    for i in range(o_ref.shape[0] // QB):
        at = slice(i * QB, (i + 1) * QB)
        for side, ref in enumerate((k_ref, v_ref)):
            scale = s_ref[0, 0, i : i + 1, side : side + 1]
            o_ref[at, side * QB : (side + 1) * QB] = (ref[at].astype(F32) * scale).astype(BF16)


def dequantize(place, blocks, scale):
    half = blocks.shape[0] // 2
    scale = scale.reshape(2, half // QB, 2, KV_HEADS).transpose(0, 3, 1, 2)
    return small(
        "dequantize",
        (1,),
        [
            pl.BlockSpec((half, QB), lambda i, p: (p[0], p[1])),
            pl.BlockSpec((half, QB), lambda i, p: (p[0], KV_HEADS + p[1])),
            pl.BlockSpec((1, 1) + scale.shape[2:], lambda i, p: (p[0], p[1], 0, 0)),
        ],
        pl.BlockSpec((half, 2 * QB), lambda i, p: (0, 0)),
        jax.ShapeDtypeStruct((half, 2 * QB), BF16),
        dequantize_kernel,
        1,
    )(place, blocks, blocks, scale)


def pack_hidden_kernel(*refs):
    o_ref = refs[-1]
    zhs = len(refs) - 1
    half = refs[0].shape[1] // 2
    for zh, ref in enumerate(refs[:-1]):
        for core in range(2):
            at = (core * zhs + zh) * half
            o_ref[0, :, at : at + half] = ref[:, core * half : (core + 1) * half]


def pack_hidden(hidden, zhs):
    tok, depth = hidden.shape
    quarter = depth // MEMBERS
    piece = quarter // zhs
    return small(
        "pack_hidden",
        (MEMBERS,),
        [pl.BlockSpec((tok, piece), lambda m, z=z: (0, z * MEMBERS + m)) for z in range(zhs)],
        pl.BlockSpec((1, tok, quarter), lambda m: (m, 0, 0)),
        jax.ShapeDtypeStruct((MEMBERS, tok, quarter), hidden.dtype),
        pack_hidden_kernel,
    )(*[hidden] * zhs)


def unpack_hidden_kernel(member_ref, *refs):
    o_ref = refs[-1]
    half = refs[0].shape[1]
    for k in range(MEMBERS):
        for core in range(2):
            at = (2 * (member_ref[0] ^ k) + core) * half
            o_ref[:, pl.ds(pl.multiple_of(at, half), half)] = refs[2 * k + core][...]


def unpack_hidden(member, pieces, zhs):
    tok, quarter = pieces[0].shape
    half = quarter // (2 * zhs)
    specs = [pl.BlockSpec((tok, half), lambda z, m, c=c: (0, c * zhs + z)) for c in range(2)]
    return small(
        "unpack_hidden",
        (zhs,),
        specs * MEMBERS,
        pl.BlockSpec((tok, 2 * half * MEMBERS), lambda z, m: (0, z)),
        jax.ShapeDtypeStruct((tok, quarter * MEMBERS), pieces[0].dtype),
        unpack_hidden_kernel,
        1,
    )(member, *[p for p in pieces for _ in range(2)])


def pack_heads_kernel(q_ref, g_ref, o_ref):
    o_ref[0, 0] = q_ref[...]
    o_ref[0, 1] = g_ref[...]


def pack_heads(queries, grad_out):
    tok, cols = queries.shape
    width = cols // MEMBERS
    block = pl.BlockSpec((tok, width), lambda m: (0, m))
    return small(
        "pack_heads",
        (MEMBERS,),
        [block, block],
        pl.BlockSpec((1, 2, tok, width), lambda m: (m, 0, 0, 0)),
        jax.ShapeDtypeStruct((MEMBERS, 2, tok, width), queries.dtype),
        pack_heads_kernel,
    )(queries, grad_out)


def unpack_heads_kernel(member_ref, *refs):
    a_ref, b_ref = refs[-2:]
    width = refs[0].shape[2]
    for k in range(MEMBERS):
        at = pl.ds(pl.multiple_of((member_ref[0] ^ k) * width, width), width)
        a_ref[:, at] = refs[k][0]
        b_ref[:, at] = refs[k][1]


def unpack_heads(member, pieces):
    _, tok, width = pieces[0].shape
    steps = 4
    rows = tok // steps
    block = pl.BlockSpec((rows, width * MEMBERS), lambda i, m: (i, 0))
    shape = jax.ShapeDtypeStruct((tok, width * MEMBERS), pieces[0].dtype)
    return small(
        "unpack_heads",
        (steps,),
        [pl.BlockSpec((2, rows, width), lambda i, m: (0, i, 0))] * MEMBERS,
        [block, block],
        [shape, shape],
        unpack_heads_kernel,
        1,
    )(member, *pieces)


def turn_kernel(x_ref, o_ref):
    o_ref[...] = x_ref[...].T


def turn(x):
    rows, cols = x.shape
    step = cols // 4
    return small(
        "turn",
        (4,),
        [pl.BlockSpec((rows, step), lambda i: (0, i))],
        pl.BlockSpec((step, rows), lambda i: (i, 0)),
        jax.ShapeDtypeStruct((cols, rows), x.dtype),
        turn_kernel,
    )(x)


def feature_block(place_ref, cores, z):
    core, zh = place_ref[1] ^ cores, place_ref[2] ^ z
    return core * MEMBERS + zh


def project_kernel(place_ref, h_ref, *refs):
    weights, (o_ref, turned) = refs[:-2], refs[-2:]
    _, half, width = weights[0].shape
    blocks = 2 * MEMBERS
    for b in range(blocks):
        at = feature_block(place_ref, b // MEMBERS, b % MEMBERS) * half
        turned[:, b * half : (b + 1) * half] = h_ref[:, pl.ds(pl.multiple_of(at, half), half)]
    rows = MEMBERS * half
    for k in range(MEMBERS):
        mine = weights[k][...].reshape(rows, width)
        theirs = weights[MEMBERS + k][...].reshape(rows, width)
        total = nn(turned[:, :rows], mine) + nn(turned[:, rows:], theirs)
        o_ref[place_ref[3] ^ k] = total


def project(place, hidden, weights):
    rows, depth = hidden.shape
    width = weights[0].shape[-1]
    whole = pl.BlockSpec(weights[0].shape, lambda i, p: (0, 0, 0))
    return pl.pallas_call(
        project_kernel,
        grid_spec=pltpu.PrefetchScalarGridSpec(
            num_scalar_prefetch=1,
            grid=(1,),
            in_specs=[pl.BlockSpec((rows, depth), lambda i, p: (0, 0))] + [whole] * len(weights),
            out_specs=pl.BlockSpec((MEMBERS, rows, width), lambda i, p: (0, 0, 0)),
            scratch_shapes=[pltpu.VMEM((rows, depth), BF16)],
        ),
        out_shape=jax.ShapeDtypeStruct((MEMBERS, rows, width), F32),
        compiler_params=pltpu.CompilerParams(vmem_limit_bytes=28 << 20),
        cost_estimate=pl.CostEstimate(
            flops=2 * rows * depth * width * MEMBERS, bytes_accessed=8 << 20, transcendentals=0
        ),
        name="project",
    )(place, hidden, *weights)


def attention_kernel(place_ref, q_ref, g_ref, far_ref, near_ref, own_ref, *refs, steps, first, last):
    if not first:
        before_ref, refs = refs[0], refs[1:]
    if last:
        outs, (dfar_ref, dnear_ref, down_ref, kv, both, acc) = refs[:steps], refs[steps:]
    else:
        outs, (acc, kv, both) = refs[:steps], refs[steps:]
    i = pl.program_id(0)
    group = own_ref.shape[0]
    tok = q_ref.shape[2]
    pairs = q_ref.shape[3] // (2 * HEAD)
    width = SPAN + tok

    @pl.when(i == 0)
    def _():
        kv[0:group] = far_ref[...]
        kv[group : 2 * group] = near_ref[...]
        kv[2 * group :] = own_ref[...]
        acc[...] = jnp.zeros_like(acc) if first else before_ref[...]

    start = pl.multiple_of(place_ref[i] * tok, tok)
    lim = place_ref[steps + i]

    def run(masked):
        keys = kv[pl.ds(start, width), 0:HEAD]
        vals = kv[pl.ds(start, width), HEAD : 2 * HEAD]
        row = lax.broadcasted_iota(jnp.int32, (tok, 2 * tok), 0)
        col = lax.broadcasted_iota(jnp.int32, (tok, 2 * tok), 1) & (tok - 1)
        for pair in range(pairs):
            a = slice(2 * pair * HEAD, (2 * pair + 1) * HEAD)
            b = slice((2 * pair + 1) * HEAD, (2 * pair + 2) * HEAD)
            q2 = jnp.concatenate([q_ref[0, 0, :, a], q_ref[0, 0, :, b]], axis=0)
            g2 = jnp.concatenate([g_ref[0, 0, :, a], g_ref[0, 0, :, b]], axis=0)
            s = nt(keys, q2)
            s = jnp.concatenate(
                [
                    jnp.where(row > col, s[:tok], NEG),
                    s[tok:SPAN],
                    jnp.where(row <= col, s[SPAN:], NEG),
                ],
                axis=0,
            )
            if masked:
                s = jnp.where(lax.broadcasted_iota(jnp.int32, s.shape, 0) >= lim, s, NEG)
            top = jnp.max(s, axis=0, keepdims=True) * (FACTOR * LOG2E)
            expd = jnp.exp2(s * (FACTOR * LOG2E) - top)
            probs = expd * (1.0 / jnp.sum(expd, axis=0, keepdims=True))
            probs_b = probs.astype(BF16)
            dprobs = nt(vals, g2)
            delta = jnp.sum(probs * dprobs, axis=0, keepdims=True)
            dscores = (probs * (dprobs - delta) * FACTOR).astype(BF16)
            acc[pl.ds(start, width), 0:HEAD] += nn(dscores, q2)
            acc[pl.ds(start, width), HEAD : 2 * HEAD] += nn(probs_b, g2)
            output = tn(probs_b, vals).astype(BF16)
            gradq = tn(dscores, keys).astype(BF16)
            both[0, :, a] = output[:tok]
            both[0, :, b] = output[tok:]
            both[1, :, a] = gradq[:tok]
            both[1, :, b] = gradq[tok:]

    @pl.when(lim <= 0)
    def _():
        run(False)

    @pl.when(lim > 0)
    def _():
        run(True)

    for step, out_ref in enumerate(outs):

        @pl.when(i == step)
        def _(out_ref=out_ref):
            out_ref[...] = both[...]

    if last:

        @pl.when(i == steps - 1)
        def _():
            dfar_ref[...] = acc[0:group].astype(dfar_ref.dtype)
            dnear_ref[...] = acc[group : 2 * group].astype(dnear_ref.dtype)
            down_ref[...] = acc[2 * group :]


def attention(place, queries, far, near, own, before=None, last=False):
    steps = place.shape[0] // 2
    first = before is None
    tok, cols = queries.shape[2:]
    group, both = own.shape
    whole = pl.BlockSpec((group, both), lambda i, p: (0, 0))
    window = pl.BlockSpec((3 * group, both), lambda i, p: (0, 0))
    out = (2, tok, cols)
    part = jax.ShapeDtypeStruct(own.shape, BF16)
    scratch = [pltpu.VMEM((3 * group, both), BF16), pltpu.VMEM(out, BF16)]
    if last:
        scratch.append(pltpu.VMEM((3 * group, both), F32))
    return pl.pallas_call(
        functools.partial(attention_kernel, steps=steps, first=first, last=last),
        grid_spec=pltpu.PrefetchScalarGridSpec(
            num_scalar_prefetch=1,
            grid=(steps,),
            in_specs=[
                pl.BlockSpec((1, 1, tok, cols), lambda i, p: (p[i], 0, 0, 0)),
                pl.BlockSpec((1, 1, tok, cols), lambda i, p: (p[i], 1, 0, 0)),
                whole,
                whole,
                whole,
            ]
            + ([] if first else [window]),
            out_specs=[pl.BlockSpec(out, lambda i, p: (0, 0, 0))] * steps
            + ([whole] * 3 if last else [window]),
            scratch_shapes=scratch,
        ),
        out_shape=[jax.ShapeDtypeStruct(out, BF16)] * steps
        + (
            [part, part, jax.ShapeDtypeStruct(own.shape, F32)]
            if last
            else [jax.ShapeDtypeStruct((3 * group, both), F32)]
        ),
        compiler_params=pltpu.CompilerParams(vmem_limit_bytes=20 << 20),
        cost_estimate=pl.CostEstimate(
            flops=7_500_000_000 * steps, bytes_accessed=2 << 20, transcendentals=1_200_000 * steps
        ),
        name="attention",
    )(*([place, queries, queries, far, near, own] + ([] if first else [before])))


def grad_hidden_kernel(place_ref, *refs):
    grads, weights, (o_ref, lined) = refs[:MEMBERS], refs[MEMBERS:-2], refs[-2:]
    _, half, width = weights[0].shape
    tok = o_ref.shape[1]
    for k, grad in enumerate(grads):
        to = place_ref[0] ^ k ^ place_ref[3]
        lined[to] = grad[...]
    line = jnp.concatenate([lined[k] for k in range(MEMBERS)], axis=1)
    for b in range(2 * MEMBERS):
        base = b // MEMBERS * MEMBERS
        rows = jnp.concatenate([weights[base + k][b % MEMBERS] for k in range(MEMBERS)], axis=1)
        total = nt(line, rows).astype(BF16)
        at = feature_block(place_ref, b // MEMBERS, b % MEMBERS) * half
        at = pl.ds(pl.multiple_of(at, half), half)
        for t in range(MEMBERS):
            o_ref[place_ref[0] ^ t, :, at] = total[t * tok : (t + 1) * tok]


def grad_hidden_quarter(place, pieces, weights):
    rows, width = pieces[0].shape
    half = weights[0].shape[1]
    depth = half * 2 * MEMBERS
    out = (MEMBERS, rows // MEMBERS, depth)
    return pl.pallas_call(
        grad_hidden_kernel,
        grid_spec=pltpu.PrefetchScalarGridSpec(
            num_scalar_prefetch=1,
            grid=(1,),
            in_specs=[pl.BlockSpec(pieces[0].shape, lambda i, p: (0, 0))] * MEMBERS
            + [pl.BlockSpec(weights[0].shape, lambda i, p: (0, 0, 0))] * len(weights),
            out_specs=pl.BlockSpec(out, lambda i, p: (0, 0, 0)),
            scratch_shapes=[pltpu.VMEM((MEMBERS, rows, width), BF16)],
        ),
        out_shape=jax.ShapeDtypeStruct(out, BF16),
        compiler_params=pltpu.CompilerParams(vmem_limit_bytes=32 << 20),
        cost_estimate=pl.CostEstimate(
            flops=2 * rows * depth * width * MEMBERS, bytes_accessed=8 << 20, transcendentals=0
        ),
        name="grad_hidden",
    )(place, *pieces, *weights)


def weight_grad_kernel(place_ref, h_ref, d0, d1, d2, d3, o_ref):
    xs, yhs, _, rows, cols = o_ref.shape
    for k, d in enumerate((d0, d1, d2, d3)):
        at = pl.multiple_of((place_ref[0] ^ k) * HEAD, HEAD)
        term = nn(h_ref[...], d[...]).astype(o_ref.dtype).reshape(xs, yhs, rows, 2 * HEAD)
        o_ref[:, :, 0, :, pl.ds(at, HEAD)] = term[..., :HEAD]
        o_ref[:, :, 0, :, pl.ds(cols // 2 + at, HEAD)] = term[..., HEAD:]


def weight_grad_share(place, turned, pieces, steps, dtype):
    feats, tokens = turned.shape
    both = pieces[0].shape[1]
    cols = both * KV_HEADS
    step = feats // (2 * steps)
    xs, yhs = lax.axis_size("x"), lax.axis_size("yh")
    out = (xs, yhs, steps, step // (xs * yhs), cols)
    return pl.pallas_call(
        weight_grad_kernel,
        grid_spec=pltpu.PrefetchScalarGridSpec(
            num_scalar_prefetch=1,
            grid=(steps,),
            in_specs=[pl.BlockSpec((step, tokens), lambda i, p: (p[1] * steps + i, 0))]
            + [pl.BlockSpec((tokens, both), lambda i, p: (0, 0))] * 4,
            out_specs=pl.BlockSpec((xs, yhs, 1) + out[3:], lambda i, p: (0, 0, i, 0, 0)),
        ),
        out_shape=jax.ShapeDtypeStruct(out, dtype),
        compiler_params=pltpu.CompilerParams(vmem_limit_bytes=14 << 20),
        cost_estimate=pl.CostEstimate(
            flops=feats * tokens * cols, bytes_accessed=5 << 20, transcendentals=0
        ),
        name="weight_grad",
    )(place, turned, *pieces)


def merge_kernel(core_ref, mine_ref, theirs_ref, o_ref):
    @pl.when(pl.program_id(0) == core_ref[0])
    def _():
        o_ref[...] = mine_ref[...].astype(F32)

    @pl.when(pl.program_id(0) != core_ref[0])
    def _():
        o_ref[...] = theirs_ref[...].astype(F32)


def merge(core, mine, theirs):
    rows, cols = mine.shape
    block = pl.BlockSpec((rows, cols), lambda i, c: (0, 0))
    return small(
        "merge",
        (2,),
        [block, block],
        pl.BlockSpec((rows, cols), lambda i, c: (i, 0)),
        jax.ShapeDtypeStruct((2 * rows, cols), F32),
        merge_kernel,
        1,
    )(core, mine, theirs)


def body(hidden, kv_blocks, kv_scale, queries, grad_out):
    tok = hidden.shape[0]
    shard, kv_cols = kv_blocks.shape
    half = shard // 2
    zh = lax.axis_index("zh")
    core = lax.axis_index("core").reshape(1)
    member = lax.axis_index(GROUP).reshape(1)
    xs, zhs = lax.axis_size("x"), lax.axis_size("zh")

    x = lax.axis_index("x").reshape(1)
    place = jnp.concatenate([member, core, zh.reshape(1), x]).astype(jnp.int32)
    rows = dequantize(jnp.concatenate([core, x]), kv_blocks, kv_scale)
    rows, hidden, queries = lax.optimization_barrier((rows, hidden, queries))
    packed, pieces = pack_hidden(hidden, zhs), pack_heads(queries, grad_out)
    rows = jnp.stack([rows] + [swapped(rows, "zh", k) for k in range(1, zhs)])
    rows, packed, pieces = lax.optimization_barrier((rows, packed, pieces))
    weights = [rows] + [swapped(rows, "x", k) for k in range(1, xs)]
    quarter = exchange(packed, GROUP).reshape(MEMBERS * tok, -1)
    quarter, pieces, weights = lax.optimization_barrier((quarter, pieces, weights))
    weights += [swapped(w, "core", 1) for w in weights]
    heads = exchange(pieces, GROUP)

    partial = project(place, quarter, weights)
    partial, heads = lax.optimization_barrier((partial, heads))
    partial = exchange(partial, GROUP)
    own = jnp.sum(partial, axis=0).astype(BF16)
    far = shifted(own, AXES, 2 * MEMBERS)
    near = shifted(own, AXES, MEMBERS)
    quarter, own = lax.optimization_barrier((quarter, own))
    turned = turn(quarter)
    far, near, turned = lax.optimization_barrier((far, near, turned))

    first = lax.axis_index(AXES) // MEMBERS * MEMBERS
    order = member ^ jnp.array([3, 1, 2, 0], jnp.int32)
    lim = jnp.maximum(0, SPAN - (first + order) * tok)

    def blocks(start, stop):
        return jnp.concatenate([order[start:stop], lim[start:stop]]).astype(jnp.int32)

    out3, before = attention(blocks(0, 1), heads, far, near, own)
    out3 = swapped(out3, GROUP, 3)
    out1, out2, before = attention(blocks(1, 3), heads, far, near, own, before)
    before, out3 = lax.optimization_barrier((before, out3))
    out1, out2 = swapped(out1, GROUP, 1), swapped(out2, GROUP, 2)
    out0, dfar, dnear, down = attention(blocks(3, 4), heads, far, near, own, before, last=True)
    outs = [out0, out1, out2, out3]
    dfar, dnear, outs = lax.optimization_barrier((dfar, dnear, outs))
    from_far = shifted(dfar, AXES, -2 * MEMBERS).astype(F32)
    from_near = shifted(dnear, AXES, -MEMBERS).astype(F32)
    all_grad = (down + from_near + from_far).astype(BF16)
    inside = down + jnp.where(zh + 1 < zhs, from_near, 0.0) + jnp.where(zh + 2 < zhs, from_far, 0.0)
    seg_grad = inside.astype(BF16)
    grads = fanned(all_grad)

    theirs = weight_grad_share(jnp.concatenate([member, 1 - core]), turned, grads, zhs, BF16)
    mine = weight_grad_share(jnp.concatenate([member, core]), turned, grads, zhs, F32)

    seg_grad, grads = lax.optimization_barrier((seg_grad, grads))
    segs = fanned(seg_grad)
    mine = (mine + swapped(theirs, "core", 1).astype(F32)).astype(BF16)
    back = grad_hidden_quarter(place, segs, weights)
    parts = exchange(mine, "x")
    backs = dealt(back)
    parts, outs, backs[:3] = lax.optimization_barrier((parts, outs, backs[:3]))
    parts = jnp.sum(parts.astype(F32), axis=0).astype(BF16)
    parts = exchange(parts.reshape((-1,) + parts.shape[2:]), ("yh", "zh"))
    summed = jnp.sum(parts.astype(F32), axis=0).astype(BF16)
    attn_out, grad_queries = unpack_heads(member, outs)
    attn_out, grad_queries, summed, backs = lax.optimization_barrier(
        (attn_out, grad_queries, summed, backs)
    )
    spread = jnp.broadcast_to(summed[None], (half // summed.shape[0],) + summed.shape)
    spread = exchange(spread, PLANE)
    grad_hidden = unpack_hidden(member, backs, zhs)
    grad_hidden, spread = lax.optimization_barrier((grad_hidden, spread))
    spread = spread.reshape(half, kv_cols)
    weight_grad = merge(core, spread, swapped(spread, "core", 1))
    return (attn_out, grad_queries, grad_hidden, weight_grad)


def solution(mesh):
    finer = Mesh(mesh.devices.reshape(SIZES), AXES)
    placed = (P(AXES, None), P(FSDP, None), P(FSDP, None), P(AXES, None), P(AXES, None))
    return jax.shard_map(
        body,
        mesh=finer,
        in_specs=placed,
        out_specs=(P(AXES, None), P(AXES, None), P(AXES, None), P(FSDP, None)),
        check_vma=False,
    )
```

```python
import functools

import jax
import jax.numpy as jnp
from jax import lax
from jax.experimental import pallas as pl
from jax.experimental.pallas import tpu as pltpu
from jax.sharding import Mesh
from jax.sharding import PartitionSpec as P

HEADS = 32
KV_HEADS = 4
HEAD = 128
QB = 128
SPAN = 1024
AXES = ("x", "yh", "core", "zh", "zl", "yl")
SIZES = (4, 2, 2, 4, 2, 2)
FSDP = ("zh", "zl", "yl")
GROUP = ("zl", "yl")
PLANE = ("x", "yh")
MEMBERS = 4

FACTOR = 1.0 / float(HEAD) ** 0.5
LOG2E = 1.4426950408889634
NEG = -1e30
F32 = jnp.float32
BF16 = jnp.bfloat16


def nt(a, b):
    return lax.dot_general(a, b, (((1,), (1,)), ((), ())), preferred_element_type=F32)


def nn(a, b):
    return lax.dot_general(a, b, (((1,), (0,)), ((), ())), preferred_element_type=F32)


def tn(a, b):
    return lax.dot_general(a, b, (((0,), (0,)), ((), ())), preferred_element_type=F32)


def shifted(block, axes, distance):
    devices = range(lax.axis_size(axes))
    route = [(i - distance, i) for i in devices if i - distance in devices]
    return lax.ppermute(block, axes, route)


def swapped(block, axes, mask):
    return lax.ppermute(block, axes, [(i, i ^ mask) for i in range(lax.axis_size(axes))])


def fanned(block):
    return [block] + [swapped(block, GROUP, k) for k in range(1, MEMBERS)]


def dealt(blocks):
    return [blocks[0]] + [swapped(blocks[k], GROUP, k) for k in range(1, MEMBERS)]


def exchange(blocks, axes):
    return lax.all_to_all(blocks, axes, split_axis=0, concat_axis=0, tiled=True)


def small(name, grid, in_specs, out_specs, out_shape, kernel, prefetch=0):
    return pl.pallas_call(
        kernel,
        grid_spec=pltpu.PrefetchScalarGridSpec(
            num_scalar_prefetch=prefetch, grid=grid, in_specs=in_specs, out_specs=out_specs
        ),
        out_shape=out_shape,
        compiler_params=pltpu.CompilerParams(vmem_limit_bytes=16 << 20),
        cost_estimate=pl.CostEstimate(flops=0, bytes_accessed=4 << 20, transcendentals=0),
        name=name,
    )


def dequantize_kernel(place_ref, k_ref, v_ref, s_ref, o_ref):
    del place_ref
    for i in range(o_ref.shape[0] // QB):
        at = slice(i * QB, (i + 1) * QB)
        for side, ref in enumerate((k_ref, v_ref)):
            scale = s_ref[0, 0, i : i + 1, side : side + 1]
            o_ref[at, side * QB : (side + 1) * QB] = (ref[at].astype(F32) * scale).astype(BF16)


def dequantize(place, blocks, scale):
    half = blocks.shape[0] // 2
    scale = scale.reshape(2, half // QB, 2, KV_HEADS).transpose(0, 3, 1, 2)
    return small(
        "dequantize",
        (1,),
        [
            pl.BlockSpec((half, QB), lambda i, p: (p[0], p[1])),
            pl.BlockSpec((half, QB), lambda i, p: (p[0], KV_HEADS + p[1])),
            pl.BlockSpec((1, 1) + scale.shape[2:], lambda i, p: (p[0], p[1], 0, 0)),
        ],
        pl.BlockSpec((half, 2 * QB), lambda i, p: (0, 0)),
        jax.ShapeDtypeStruct((half, 2 * QB), BF16),
        dequantize_kernel,
        1,
    )(place, blocks, blocks, scale)


def pack_hidden_kernel(*refs):
    o_ref = refs[-1]
    zhs = len(refs) - 1
    half = refs[0].shape[1] // 2
    for zh, ref in enumerate(refs[:-1]):
        for core in range(2):
            at = (core * zhs + zh) * half
            o_ref[0, :, at : at + half] = ref[:, core * half : (core + 1) * half]


def pack_hidden(hidden, zhs):
    tok, depth = hidden.shape
    quarter = depth // MEMBERS
    piece = quarter // zhs
    return small(
        "pack_hidden",
        (MEMBERS,),
        [pl.BlockSpec((tok, piece), lambda m, z=z: (0, z * MEMBERS + m)) for z in range(zhs)],
        pl.BlockSpec((1, tok, quarter), lambda m: (m, 0, 0)),
        jax.ShapeDtypeStruct((MEMBERS, tok, quarter), hidden.dtype),
        pack_hidden_kernel,
    )(*[hidden] * zhs)


def unpack_hidden_kernel(member_ref, *refs):
    o_ref = refs[-1]
    half = refs[0].shape[1]
    for k in range(MEMBERS):
        for core in range(2):
            at = (2 * (member_ref[0] ^ k) + core) * half
            o_ref[:, pl.ds(pl.multiple_of(at, half), half)] = refs[2 * k + core][...]


def unpack_hidden(member, pieces, zhs):
    tok, quarter = pieces[0].shape
    half = quarter // (2 * zhs)
    specs = [pl.BlockSpec((tok, half), lambda z, m, c=c: (0, c * zhs + z)) for c in range(2)]
    return small(
        "unpack_hidden",
        (zhs,),
        specs * MEMBERS,
        pl.BlockSpec((tok, 2 * half * MEMBERS), lambda z, m: (0, z)),
        jax.ShapeDtypeStruct((tok, quarter * MEMBERS), pieces[0].dtype),
        unpack_hidden_kernel,
        1,
    )(member, *[p for p in pieces for _ in range(2)])


def pack_heads_kernel(member_ref, q_ref, g_ref, o_ref):
    del member_ref
    o_ref[0, 0] = q_ref[...]
    o_ref[0, 1] = g_ref[...]


def pack_heads(member, queries, grad_out):
    tok, cols = queries.shape
    width = cols // MEMBERS
    block = pl.BlockSpec((tok, width), lambda k, m: (0, k ^ m[0]))
    return small(
        "pack_heads",
        (MEMBERS,),
        [block, block],
        pl.BlockSpec((1, 2, tok, width), lambda k, m: (k, 0, 0, 0)),
        jax.ShapeDtypeStruct((MEMBERS, 2, tok, width), queries.dtype),
        pack_heads_kernel,
        1,
    )(member, queries, grad_out)


def unpack_heads_kernel(member_ref, *refs):
    a_ref, b_ref = refs[-2:]
    width = refs[0].shape[2]
    for k in range(MEMBERS):
        at = pl.ds(pl.multiple_of((member_ref[0] ^ k) * width, width), width)
        a_ref[:, at] = refs[k][0]
        b_ref[:, at] = refs[k][1]


def unpack_heads(member, pieces):
    _, tok, width = pieces[0].shape
    steps = 4
    rows = tok // steps
    block = pl.BlockSpec((rows, width * MEMBERS), lambda i, m: (i, 0))
    shape = jax.ShapeDtypeStruct((tok, width * MEMBERS), pieces[0].dtype)
    return small(
        "unpack_heads",
        (steps,),
        [pl.BlockSpec((2, rows, width), lambda i, m: (0, i, 0))] * MEMBERS,
        [block, block],
        [shape, shape],
        unpack_heads_kernel,
        1,
    )(member, *pieces)


def turn_kernel(x_ref, o_ref):
    o_ref[...] = x_ref[...].T


def turn(x):
    rows, cols = x.shape
    step = cols // 4
    return small(
        "turn",
        (4,),
        [pl.BlockSpec((rows, step), lambda i: (0, i))],
        pl.BlockSpec((step, rows), lambda i: (i, 0)),
        jax.ShapeDtypeStruct((cols, rows), x.dtype),
        turn_kernel,
    )(x)


def feature_block(place_ref, cores, z):
    core, zh = place_ref[1] ^ cores, place_ref[2] ^ z
    return core * MEMBERS + zh


def project_kernel(place_ref, h_ref, *refs):
    weights, (o_ref, turned) = refs[:-2], refs[-2:]
    _, half, width = weights[0].shape
    blocks = 2 * MEMBERS
    for b in range(blocks):
        at = feature_block(place_ref, b // MEMBERS, b % MEMBERS) * half
        turned[:, b * half : (b + 1) * half] = h_ref[:, pl.ds(pl.multiple_of(at, half), half)]
    rows = MEMBERS * half
    for k in range(MEMBERS):
        mine = weights[k][...].reshape(rows, width)
        theirs = weights[MEMBERS + k][...].reshape(rows, width)
        total = nn(turned[:, :rows], mine) + nn(turned[:, rows:], theirs)
        o_ref[place_ref[3] ^ k] = total


def project(place, hidden, weights):
    rows, depth = hidden.shape
    width = weights[0].shape[-1]
    whole = pl.BlockSpec(weights[0].shape, lambda i, p: (0, 0, 0))
    return pl.pallas_call(
        project_kernel,
        grid_spec=pltpu.PrefetchScalarGridSpec(
            num_scalar_prefetch=1,
            grid=(1,),
            in_specs=[pl.BlockSpec((rows, depth), lambda i, p: (0, 0))] + [whole] * len(weights),
            out_specs=pl.BlockSpec((MEMBERS, rows, width), lambda i, p: (0, 0, 0)),
            scratch_shapes=[pltpu.VMEM((rows, depth), BF16)],
        ),
        out_shape=jax.ShapeDtypeStruct((MEMBERS, rows, width), F32),
        compiler_params=pltpu.CompilerParams(vmem_limit_bytes=28 << 20),
        cost_estimate=pl.CostEstimate(
            flops=2 * rows * depth * width * MEMBERS, bytes_accessed=8 << 20, transcendentals=0
        ),
        name="project",
    )(place, hidden, *weights)


def attention_kernel(place_ref, far_ref, near_ref, own_ref, *refs, steps, first, last):
    pieces, refs = refs[:steps], refs[steps:]
    if not first:
        before_ref, refs = refs[0], refs[1:]
    if last:
        outs, (dfar_ref, dnear_ref, down_ref, kv, both, taken, acc) = refs[:steps], refs[steps:]
    else:
        outs, (acc, kv, both, taken) = refs[:steps], refs[steps:]
    i = pl.program_id(0)
    group = own_ref.shape[0]
    tok, cols = pieces[0].shape[1:]
    pairs = cols // (2 * HEAD)
    width = SPAN + tok

    @pl.when(i == 0)
    def _():
        kv[0:group] = far_ref[...]
        kv[group : 2 * group] = near_ref[...]
        kv[2 * group :] = own_ref[...]
        acc[...] = jnp.zeros_like(acc) if first else before_ref[...]

    for step, piece in enumerate(pieces):

        @pl.when(i == step)
        def _(piece=piece):
            taken[...] = piece[...]

    start = pl.multiple_of(place_ref[i] * tok, tok)
    lim = place_ref[steps + i]

    def run(masked):
        keys = kv[pl.ds(start, width), 0:HEAD]
        vals = kv[pl.ds(start, width), HEAD : 2 * HEAD]
        row = lax.broadcasted_iota(jnp.int32, (tok, 2 * tok), 0)
        col = lax.broadcasted_iota(jnp.int32, (tok, 2 * tok), 1) & (tok - 1)
        for pair in range(pairs):
            a = slice(2 * pair * HEAD, (2 * pair + 1) * HEAD)
            b = slice((2 * pair + 1) * HEAD, (2 * pair + 2) * HEAD)
            q2 = jnp.concatenate([taken[0, :, a], taken[0, :, b]], axis=0)
            g2 = jnp.concatenate([taken[1, :, a], taken[1, :, b]], axis=0)
            s = nt(keys, q2)
            s = jnp.concatenate(
                [
                    jnp.where(row > col, s[:tok], NEG),
                    s[tok:SPAN],
                    jnp.where(row <= col, s[SPAN:], NEG),
                ],
                axis=0,
            )
            if masked:
                s = jnp.where(lax.broadcasted_iota(jnp.int32, s.shape, 0) >= lim, s, NEG)
            top = jnp.max(s, axis=0, keepdims=True) * (FACTOR * LOG2E)
            expd = jnp.exp2(s * (FACTOR * LOG2E) - top)
            probs = expd * (1.0 / jnp.sum(expd, axis=0, keepdims=True))
            probs_b = probs.astype(BF16)
            dprobs = nt(vals, g2)
            delta = jnp.sum(probs * dprobs, axis=0, keepdims=True)
            dscores = (probs * (dprobs - delta) * FACTOR).astype(BF16)
            acc[pl.ds(start, width), 0:HEAD] += nn(dscores, q2)
            acc[pl.ds(start, width), HEAD : 2 * HEAD] += nn(probs_b, g2)
            output = tn(probs_b, vals).astype(BF16)
            gradq = tn(dscores, keys).astype(BF16)
            both[0, :, a] = output[:tok]
            both[0, :, b] = output[tok:]
            both[1, :, a] = gradq[:tok]
            both[1, :, b] = gradq[tok:]

    @pl.when(lim <= 0)
    def _():
        run(False)

    @pl.when(lim > 0)
    def _():
        run(True)

    for step, out_ref in enumerate(outs):

        @pl.when(i == step)
        def _(out_ref=out_ref):
            out_ref[...] = both[...]

    if last:

        @pl.when(i == steps - 1)
        def _():
            dfar_ref[...] = acc[0:group].astype(dfar_ref.dtype)
            dnear_ref[...] = acc[group : 2 * group].astype(dnear_ref.dtype)
            down_ref[...] = acc[2 * group :]


def attention(place, pieces, far, near, own, before=None, last=False):
    steps = place.shape[0] // 2
    first = before is None
    out = pieces[0].shape
    group, both = own.shape
    whole = pl.BlockSpec((group, both), lambda i, p: (0, 0))
    window = pl.BlockSpec((3 * group, both), lambda i, p: (0, 0))
    piece = pl.BlockSpec(out, lambda i, p: (0, 0, 0))
    part = jax.ShapeDtypeStruct(own.shape, BF16)
    scratch = [pltpu.VMEM((3 * group, both), BF16)] + [pltpu.VMEM(out, BF16)] * 2
    if last:
        scratch.append(pltpu.VMEM((3 * group, both), F32))
    return pl.pallas_call(
        functools.partial(attention_kernel, steps=steps, first=first, last=last),
        grid_spec=pltpu.PrefetchScalarGridSpec(
            num_scalar_prefetch=1,
            grid=(steps,),
            in_specs=[
                whole,
                whole,
                whole,
            ]
            + [piece] * steps
            + ([] if first else [window]),
            out_specs=[piece] * steps
            + ([whole] * 3 if last else [window]),
            scratch_shapes=scratch,
        ),
        out_shape=[jax.ShapeDtypeStruct(out, BF16)] * steps
        + (
            [part, part, jax.ShapeDtypeStruct(own.shape, F32)]
            if last
            else [jax.ShapeDtypeStruct((3 * group, both), F32)]
        ),
        compiler_params=pltpu.CompilerParams(vmem_limit_bytes=20 << 20),
        cost_estimate=pl.CostEstimate(
            flops=7_500_000_000 * steps, bytes_accessed=2 << 20, transcendentals=1_200_000 * steps
        ),
        name="attention",
    )(*([place, far, near, own] + pieces + ([] if first else [before])))


def grad_hidden_kernel(place_ref, *refs):
    grads, weights, (o_ref, lined) = refs[:MEMBERS], refs[MEMBERS:-2], refs[-2:]
    _, half, width = weights[0].shape
    tok = o_ref.shape[1]
    for k, grad in enumerate(grads):
        to = place_ref[0] ^ k ^ place_ref[3]
        lined[to] = grad[...]
    line = jnp.concatenate([lined[k] for k in range(MEMBERS)], axis=1)
    for b in range(2 * MEMBERS):
        base = b // MEMBERS * MEMBERS
        rows = jnp.concatenate([weights[base + k][b % MEMBERS] for k in range(MEMBERS)], axis=1)
        total = nt(line, rows).astype(BF16)
        at = feature_block(place_ref, b // MEMBERS, b % MEMBERS) * half
        at = pl.ds(pl.multiple_of(at, half), half)
        for t in range(MEMBERS):
            o_ref[place_ref[0] ^ t, :, at] = total[t * tok : (t + 1) * tok]


def grad_hidden_quarter(place, pieces, weights):
    rows, width = pieces[0].shape
    half = weights[0].shape[1]
    depth = half * 2 * MEMBERS
    out = (MEMBERS, rows // MEMBERS, depth)
    return pl.pallas_call(
        grad_hidden_kernel,
        grid_spec=pltpu.PrefetchScalarGridSpec(
            num_scalar_prefetch=1,
            grid=(1,),
            in_specs=[pl.BlockSpec(pieces[0].shape, lambda i, p: (0, 0))] * MEMBERS
            + [pl.BlockSpec(weights[0].shape, lambda i, p: (0, 0, 0))] * len(weights),
            out_specs=pl.BlockSpec(out, lambda i, p: (0, 0, 0)),
            scratch_shapes=[pltpu.VMEM((MEMBERS, rows, width), BF16)],
        ),
        out_shape=jax.ShapeDtypeStruct(out, BF16),
        compiler_params=pltpu.CompilerParams(vmem_limit_bytes=32 << 20),
        cost_estimate=pl.CostEstimate(
            flops=2 * rows * depth * width * MEMBERS, bytes_accessed=8 << 20, transcendentals=0
        ),
        name="grad_hidden",
    )(place, *pieces, *weights)


def weight_grad_kernel(place_ref, h_ref, d0, d1, d2, d3, o_ref):
    xs, yhs, _, rows, cols = o_ref.shape
    for k, d in enumerate((d0, d1, d2, d3)):
        at = pl.multiple_of((place_ref[0] ^ k) * HEAD, HEAD)
        term = nn(h_ref[...], d[...]).astype(o_ref.dtype).reshape(xs, yhs, rows, 2 * HEAD)
        o_ref[:, :, 0, :, pl.ds(at, HEAD)] = term[..., :HEAD]
        o_ref[:, :, 0, :, pl.ds(cols // 2 + at, HEAD)] = term[..., HEAD:]


def weight_grad_share(place, turned, pieces, steps, dtype):
    feats, tokens = turned.shape
    both = pieces[0].shape[1]
    cols = both * KV_HEADS
    step = feats // (2 * steps)
    xs, yhs = lax.axis_size("x"), lax.axis_size("yh")
    out = (xs, yhs, steps, step // (xs * yhs), cols)
    return pl.pallas_call(
        weight_grad_kernel,
        grid_spec=pltpu.PrefetchScalarGridSpec(
            num_scalar_prefetch=1,
            grid=(steps,),
            in_specs=[pl.BlockSpec((step, tokens), lambda i, p: (p[1] * steps + i, 0))]
            + [pl.BlockSpec((tokens, both), lambda i, p: (0, 0))] * 4,
            out_specs=pl.BlockSpec((xs, yhs, 1) + out[3:], lambda i, p: (0, 0, i, 0, 0)),
        ),
        out_shape=jax.ShapeDtypeStruct(out, dtype),
        compiler_params=pltpu.CompilerParams(vmem_limit_bytes=14 << 20),
        cost_estimate=pl.CostEstimate(
            flops=feats * tokens * cols, bytes_accessed=5 << 20, transcendentals=0
        ),
        name="weight_grad",
    )(place, turned, *pieces)


def total_kernel(x_ref, o_ref):
    total = x_ref[0].astype(F32)
    for k in range(1, x_ref.shape[0]):
        total = total + x_ref[k].astype(F32)
    o_ref[...] = total.astype(o_ref.dtype)


def total(x, steps):
    count, blocks = x.shape[:2]
    size = blocks // steps
    tail = x.shape[2:]
    return small(
        "total",
        (steps,),
        [pl.BlockSpec((count, size) + tail, lambda i: (0, i, 0, 0))],
        pl.BlockSpec((size,) + tail, lambda i: (i, 0, 0)),
        jax.ShapeDtypeStruct((blocks,) + tail, x.dtype),
        total_kernel,
    )(x)


def merge_kernel(core_ref, mine_ref, theirs_ref, o_ref):
    @pl.when(pl.program_id(0) == core_ref[0])
    def _():
        o_ref[...] = mine_ref[...].astype(F32)

    @pl.when(pl.program_id(0) != core_ref[0])
    def _():
        o_ref[...] = theirs_ref[...].astype(F32)


def merge(core, mine, theirs):
    rows, cols = mine.shape
    block = pl.BlockSpec((rows, cols), lambda i, c: (0, 0))
    return small(
        "merge",
        (2,),
        [block, block],
        pl.BlockSpec((rows, cols), lambda i, c: (i, 0)),
        jax.ShapeDtypeStruct((2 * rows, cols), F32),
        merge_kernel,
        1,
    )(core, mine, theirs)


def body(hidden, kv_blocks, kv_scale, queries, grad_out):
    tok = hidden.shape[0]
    shard, kv_cols = kv_blocks.shape
    half = shard // 2
    zh = lax.axis_index("zh")
    core = lax.axis_index("core").reshape(1)
    member = lax.axis_index(GROUP).reshape(1)
    xs, zhs = lax.axis_size("x"), lax.axis_size("zh")

    x = lax.axis_index("x").reshape(1)
    place = jnp.concatenate([member, core, zh.reshape(1), x]).astype(jnp.int32)
    rows = dequantize(jnp.concatenate([core, x]), kv_blocks, kv_scale)
    rows, hidden, queries = lax.optimization_barrier((rows, hidden, queries))
    packed, pieces = pack_hidden(hidden, zhs), pack_heads(member, queries, grad_out)
    rows = jnp.stack([rows] + [swapped(rows, "zh", k) for k in range(1, zhs)])
    rows, packed, pieces = lax.optimization_barrier((rows, packed, pieces))
    weights = [rows] + [swapped(rows, "x", k) for k in range(1, xs)]
    quarter = exchange(packed, GROUP).reshape(MEMBERS * tok, -1)
    quarter, pieces, weights = lax.optimization_barrier((quarter, pieces, weights))
    weights += [swapped(w, "core", 1) for w in weights]
    head3, head2 = swapped(pieces[3], GROUP, 3), swapped(pieces[2], GROUP, 2)

    partial = project(place, quarter, weights)
    partial, head3, head2, pieces = lax.optimization_barrier((partial, head3, head2, pieces))
    partial = exchange(partial, GROUP)
    own = jnp.sum(partial, axis=0).astype(BF16)
    far = shifted(own, AXES, 2 * MEMBERS)
    near = shifted(own, AXES, MEMBERS)
    quarter, own = lax.optimization_barrier((quarter, own))
    turned = turn(quarter)
    head1 = swapped(pieces[1], GROUP, 1)
    far, near, turned, head1 = lax.optimization_barrier((far, near, turned, head1))

    first = lax.axis_index(AXES) // MEMBERS * MEMBERS
    order = member ^ jnp.array([3, 1, 2, 0], jnp.int32)
    lim = jnp.maximum(0, SPAN - (first + order) * tok)

    def blocks(start, stop):
        return jnp.concatenate([order[start:stop], lim[start:stop]]).astype(jnp.int32)

    out3, before = attention(blocks(0, 1), [head3], far, near, own)
    out3 = swapped(out3, GROUP, 3)
    out1, out2, before = attention(blocks(1, 3), [head1, head2], far, near, own, before)
    before, out3 = lax.optimization_barrier((before, out3))
    out1, out2 = swapped(out1, GROUP, 1), swapped(out2, GROUP, 2)
    out0, dfar, dnear, down = attention(
        blocks(3, 4), [pieces[0]], far, near, own, before, last=True
    )
    outs = [out0, out1, out2, out3]
    dfar, dnear, outs = lax.optimization_barrier((dfar, dnear, outs))
    from_far = shifted(dfar, AXES, -2 * MEMBERS).astype(F32)
    from_near = shifted(dnear, AXES, -MEMBERS).astype(F32)
    all_grad = (down + from_near + from_far).astype(BF16)
    inside = down + jnp.where(zh + 1 < zhs, from_near, 0.0) + jnp.where(zh + 2 < zhs, from_far, 0.0)
    seg_grad = inside.astype(BF16)
    grads = fanned(all_grad)

    theirs = weight_grad_share(jnp.concatenate([member, 1 - core]), turned, grads, zhs, BF16)
    mine = weight_grad_share(jnp.concatenate([member, core]), turned, grads, zhs, F32)

    seg_grad, grads = lax.optimization_barrier((seg_grad, grads))
    segs = fanned(seg_grad)
    mine = (mine + swapped(theirs, "core", 1).astype(F32)).astype(BF16)
    back = grad_hidden_quarter(place, segs, weights)
    parts = exchange(mine, "x")
    backs = dealt(back)
    parts, outs, backs[:3] = lax.optimization_barrier((parts, outs, backs[:3]))
    parts = total(parts.reshape((xs, -1) + parts.shape[3:]), 4)
    parts = exchange(parts, ("yh", "zh"))
    summed = jnp.sum(parts.astype(F32), axis=0).astype(BF16)
    attn_out, grad_queries = unpack_heads(member, outs)
    attn_out, grad_queries, summed = lax.optimization_barrier((attn_out, grad_queries, summed))
    spread = jnp.broadcast_to(summed[None], (half // summed.shape[0],) + summed.shape)
    spread = exchange(spread, PLANE)
    backs, spread = lax.optimization_barrier((backs, spread))
    grad_hidden = unpack_hidden(member, backs, zhs)
    spread = spread.reshape(half, kv_cols)
    weight_grad = merge(core, spread, swapped(spread, "core", 1))
    return (attn_out, grad_queries, grad_hidden, weight_grad)


def solution(mesh):
    finer = Mesh(mesh.devices.reshape(SIZES), AXES)
    placed = (P(AXES, None), P(FSDP, None), P(FSDP, None), P(AXES, None), P(AXES, None))
    return jax.shard_map(
        body,
        mesh=finer,
        in_specs=placed,
        out_specs=(P(AXES, None), P(AXES, None), P(AXES, None), P(FSDP, None)),
        check_vma=False,
    )
```

```python
import functools

import jax
import jax.numpy as jnp
from jax import lax
from jax.experimental import pallas as pl
from jax.experimental.pallas import tpu as pltpu
from jax.sharding import Mesh
from jax.sharding import PartitionSpec as P

HEADS = 32
KV_HEADS = 4
HEAD = 128
QB = 128
SPAN = 1024
AXES = ("x", "yh", "core", "zh", "zl", "yl")
SIZES = (4, 2, 2, 4, 2, 2)
FSDP = ("zh", "zl", "yl")
GROUP = ("zl", "yl")
PLANE = ("x", "yh")
MEMBERS = 4

FACTOR = 1.0 / float(HEAD) ** 0.5
LOG2E = 1.4426950408889634
NEG = -1e30
F32 = jnp.float32
BF16 = jnp.bfloat16


def nt(a, b):
    return lax.dot_general(a, b, (((1,), (1,)), ((), ())), preferred_element_type=F32)


def nn(a, b):
    return lax.dot_general(a, b, (((1,), (0,)), ((), ())), preferred_element_type=F32)


def tn(a, b):
    return lax.dot_general(a, b, (((0,), (0,)), ((), ())), preferred_element_type=F32)


def shifted(block, axes, distance):
    devices = range(lax.axis_size(axes))
    route = [(i - distance, i) for i in devices if i - distance in devices]
    return lax.ppermute(block, axes, route)


def swapped(block, axes, mask):
    return lax.ppermute(block, axes, [(i, i ^ mask) for i in range(lax.axis_size(axes))])


def fanned(block):
    return [block] + [swapped(block, GROUP, k) for k in range(1, MEMBERS)]


def dealt(blocks):
    return [blocks[0]] + [swapped(blocks[k], GROUP, k) for k in range(1, MEMBERS)]


def exchange(blocks, axes):
    return lax.all_to_all(blocks, axes, split_axis=0, concat_axis=0, tiled=True)


def small(name, grid, in_specs, out_specs, out_shape, kernel, prefetch=0):
    return pl.pallas_call(
        kernel,
        grid_spec=pltpu.PrefetchScalarGridSpec(
            num_scalar_prefetch=prefetch, grid=grid, in_specs=in_specs, out_specs=out_specs
        ),
        out_shape=out_shape,
        compiler_params=pltpu.CompilerParams(vmem_limit_bytes=16 << 20),
        cost_estimate=pl.CostEstimate(flops=0, bytes_accessed=4 << 20, transcendentals=0),
        name=name,
    )


def dequantize_kernel(place_ref, k_ref, v_ref, s_ref, o_ref):
    del place_ref
    for i in range(o_ref.shape[0] // QB):
        at = slice(i * QB, (i + 1) * QB)
        for side, ref in enumerate((k_ref, v_ref)):
            scale = s_ref[0, 0, i : i + 1, side : side + 1]
            o_ref[at, side * QB : (side + 1) * QB] = (ref[at].astype(F32) * scale).astype(BF16)


def dequantize(place, blocks, scale):
    half = blocks.shape[0] // 2
    scale = scale.reshape(2, half // QB, 2, KV_HEADS).transpose(0, 3, 1, 2)
    return small(
        "dequantize",
        (1,),
        [
            pl.BlockSpec((half, QB), lambda i, p: (p[0], p[1])),
            pl.BlockSpec((half, QB), lambda i, p: (p[0], KV_HEADS + p[1])),
            pl.BlockSpec((1, 1) + scale.shape[2:], lambda i, p: (p[0], p[1], 0, 0)),
        ],
        pl.BlockSpec((half, 2 * QB), lambda i, p: (0, 0)),
        jax.ShapeDtypeStruct((half, 2 * QB), BF16),
        dequantize_kernel,
        1,
    )(place, blocks, blocks, scale)


def pack_hidden_kernel(*refs):
    o_ref = refs[-1]
    zhs = len(refs) - 1
    half = refs[0].shape[1] // 2
    for zh, ref in enumerate(refs[:-1]):
        for core in range(2):
            at = (core * zhs + zh) * half
            o_ref[0, :, at : at + half] = ref[:, core * half : (core + 1) * half]


def pack_hidden(hidden, zhs):
    tok, depth = hidden.shape
    quarter = depth // MEMBERS
    piece = quarter // zhs
    return small(
        "pack_hidden",
        (MEMBERS,),
        [pl.BlockSpec((tok, piece), lambda m, z=z: (0, z * MEMBERS + m)) for z in range(zhs)],
        pl.BlockSpec((1, tok, quarter), lambda m: (m, 0, 0)),
        jax.ShapeDtypeStruct((MEMBERS, tok, quarter), hidden.dtype),
        pack_hidden_kernel,
    )(*[hidden] * zhs)


def unpack_hidden_kernel(member_ref, *refs):
    o_ref = refs[-1]
    half = refs[0].shape[1]
    for k in range(MEMBERS):
        for core in range(2):
            at = (2 * (member_ref[0] ^ k) + core) * half
            o_ref[:, pl.ds(pl.multiple_of(at, half), half)] = refs[2 * k + core][...]


def unpack_hidden(member, pieces, zhs):
    tok, quarter = pieces[0].shape
    half = quarter // (2 * zhs)
    specs = [pl.BlockSpec((tok, half), lambda z, m, c=c: (0, c * zhs + z)) for c in range(2)]
    return small(
        "unpack_hidden",
        (zhs,),
        specs * MEMBERS,
        pl.BlockSpec((tok, 2 * half * MEMBERS), lambda z, m: (0, z)),
        jax.ShapeDtypeStruct((tok, quarter * MEMBERS), pieces[0].dtype),
        unpack_hidden_kernel,
        1,
    )(member, *[p for p in pieces for _ in range(2)])


def pack_heads_kernel(member_ref, q_ref, g_ref, o_ref):
    del member_ref
    o_ref[0, 0] = q_ref[...]
    o_ref[0, 1] = g_ref[...]


def pack_heads(member, queries, grad_out):
    tok, cols = queries.shape
    width = cols // MEMBERS
    block = pl.BlockSpec((tok, width), lambda k, m: (0, k ^ m[0]))
    return small(
        "pack_heads",
        (MEMBERS,),
        [block, block],
        pl.BlockSpec((1, 2, tok, width), lambda k, m: (k, 0, 0, 0)),
        jax.ShapeDtypeStruct((MEMBERS, 2, tok, width), queries.dtype),
        pack_heads_kernel,
        1,
    )(member, queries, grad_out)


def unpack_heads_kernel(member_ref, *refs):
    a_ref, b_ref = refs[-2:]
    width = refs[0].shape[2]
    for k in range(MEMBERS):
        at = pl.ds(pl.multiple_of((member_ref[0] ^ k) * width, width), width)
        a_ref[:, at] = refs[k][0]
        b_ref[:, at] = refs[k][1]


def unpack_heads(member, pieces):
    _, tok, width = pieces[0].shape
    steps = 4
    rows = tok // steps
    block = pl.BlockSpec((rows, width * MEMBERS), lambda i, m: (i, 0))
    shape = jax.ShapeDtypeStruct((tok, width * MEMBERS), pieces[0].dtype)
    return small(
        "unpack_heads",
        (steps,),
        [pl.BlockSpec((2, rows, width), lambda i, m: (0, i, 0))] * MEMBERS,
        [block, block],
        [shape, shape],
        unpack_heads_kernel,
        1,
    )(member, *pieces)


def turn_kernel(x_ref, o_ref):
    o_ref[...] = x_ref[...].T


def turn(x):
    rows, cols = x.shape
    step = cols // 4
    return small(
        "turn",
        (4,),
        [pl.BlockSpec((rows, step), lambda i: (0, i))],
        pl.BlockSpec((step, rows), lambda i: (i, 0)),
        jax.ShapeDtypeStruct((cols, rows), x.dtype),
        turn_kernel,
    )(x)


def feature_block(place_ref, cores, z):
    core, zh = place_ref[1] ^ cores, place_ref[2] ^ z
    return core * MEMBERS + zh


def project_kernel(place_ref, h_ref, *refs):
    weights, (o_ref, turned) = refs[:-2], refs[-2:]
    _, half, width = weights[0].shape
    blocks = 2 * MEMBERS
    for b in range(blocks):
        at = feature_block(place_ref, b // MEMBERS, b % MEMBERS) * half
        turned[:, b * half : (b + 1) * half] = h_ref[:, pl.ds(pl.multiple_of(at, half), half)]
    rows = MEMBERS * half
    for k in range(MEMBERS):
        mine = weights[k][...].reshape(rows, width)
        theirs = weights[MEMBERS + k][...].reshape(rows, width)
        total = nn(turned[:, :rows], mine) + nn(turned[:, rows:], theirs)
        o_ref[place_ref[3] ^ k] = total


def project(place, hidden, weights):
    rows, depth = hidden.shape
    width = weights[0].shape[-1]
    whole = pl.BlockSpec(weights[0].shape, lambda i, p: (0, 0, 0))
    return pl.pallas_call(
        project_kernel,
        grid_spec=pltpu.PrefetchScalarGridSpec(
            num_scalar_prefetch=1,
            grid=(1,),
            in_specs=[pl.BlockSpec((rows, depth), lambda i, p: (0, 0))] + [whole] * len(weights),
            out_specs=pl.BlockSpec((MEMBERS, rows, width), lambda i, p: (0, 0, 0)),
            scratch_shapes=[pltpu.VMEM((rows, depth), BF16)],
        ),
        out_shape=jax.ShapeDtypeStruct((MEMBERS, rows, width), F32),
        compiler_params=pltpu.CompilerParams(vmem_limit_bytes=28 << 20),
        cost_estimate=pl.CostEstimate(
            flops=2 * rows * depth * width * MEMBERS, bytes_accessed=8 << 20, transcendentals=0
        ),
        name="project",
    )(place, hidden, *weights)


def attention_kernel(place_ref, far_ref, near_ref, own_ref, *refs, steps, first, last):
    pieces, refs = refs[:steps], refs[steps:]
    if not first:
        before_ref, refs = refs[0], refs[1:]
    if last:
        outs, (dfar_ref, dnear_ref, down_ref, kv, both, taken, acc) = refs[:steps], refs[steps:]
    else:
        outs, (acc, kv, both, taken) = refs[:steps], refs[steps:]
    i = pl.program_id(0)
    group = own_ref.shape[0]
    tok, cols = pieces[0].shape[1:]
    pairs = cols // (2 * HEAD)
    width = SPAN + tok

    @pl.when(i == 0)
    def _():
        kv[0:group] = far_ref[...]
        kv[group : 2 * group] = near_ref[...]
        kv[2 * group :] = own_ref[...]
        acc[...] = jnp.zeros_like(acc) if first else before_ref[...]

    for step, piece in enumerate(pieces):

        @pl.when(i == step)
        def _(piece=piece):
            taken[...] = piece[...]

    start = pl.multiple_of(place_ref[i] * tok, tok)
    lim = place_ref[steps + i]

    def run(masked):
        keys = kv[pl.ds(start, width), 0:HEAD]
        vals = kv[pl.ds(start, width), HEAD : 2 * HEAD]
        row = lax.broadcasted_iota(jnp.int32, (tok, 2 * tok), 0)
        col = lax.broadcasted_iota(jnp.int32, (tok, 2 * tok), 1) & (tok - 1)
        for pair in range(pairs):
            a = slice(2 * pair * HEAD, (2 * pair + 1) * HEAD)
            b = slice((2 * pair + 1) * HEAD, (2 * pair + 2) * HEAD)
            q2 = jnp.concatenate([taken[0, :, a], taken[0, :, b]], axis=0)
            g2 = jnp.concatenate([taken[1, :, a], taken[1, :, b]], axis=0)
            s = nt(keys, q2)
            s = jnp.concatenate(
                [
                    jnp.where(row > col, s[:tok], NEG),
                    s[tok:SPAN],
                    jnp.where(row <= col, s[SPAN:], NEG),
                ],
                axis=0,
            )
            if masked:
                s = jnp.where(lax.broadcasted_iota(jnp.int32, s.shape, 0) >= lim, s, NEG)
            top = jnp.max(s, axis=0, keepdims=True) * (FACTOR * LOG2E)
            expd = jnp.exp2(s * (FACTOR * LOG2E) - top)
            probs = expd * (1.0 / jnp.sum(expd, axis=0, keepdims=True))
            probs_b = probs.astype(BF16)
            dprobs = nt(vals, g2)
            delta = jnp.sum(probs * dprobs, axis=0, keepdims=True)
            dscores = (probs * (dprobs - delta) * FACTOR).astype(BF16)
            acc[pl.ds(start, width), 0:HEAD] += nn(dscores, q2)
            acc[pl.ds(start, width), HEAD : 2 * HEAD] += nn(probs_b, g2)
            output = tn(probs_b, vals).astype(BF16)
            gradq = tn(dscores, keys).astype(BF16)
            both[0, :, a] = output[:tok]
            both[0, :, b] = output[tok:]
            both[1, :, a] = gradq[:tok]
            both[1, :, b] = gradq[tok:]

    @pl.when(lim <= 0)
    def _():
        run(False)

    @pl.when(lim > 0)
    def _():
        run(True)

    for step, out_ref in enumerate(outs):

        @pl.when(i == step)
        def _(out_ref=out_ref):
            out_ref[...] = both[...]

    if last:

        @pl.when(i == steps - 1)
        def _():
            dfar_ref[...] = acc[0:group].astype(dfar_ref.dtype)
            dnear_ref[...] = acc[group : 2 * group].astype(dnear_ref.dtype)
            down_ref[...] = acc[2 * group :]


def attention(place, pieces, far, near, own, before=None, last=False):
    steps = place.shape[0] // 2
    first = before is None
    out = pieces[0].shape
    group, both = own.shape
    whole = pl.BlockSpec((group, both), lambda i, p: (0, 0))
    window = pl.BlockSpec((3 * group, both), lambda i, p: (0, 0))
    piece = pl.BlockSpec(out, lambda i, p: (0, 0, 0))
    part = jax.ShapeDtypeStruct(own.shape, BF16)
    scratch = [pltpu.VMEM((3 * group, both), BF16)] + [pltpu.VMEM(out, BF16)] * 2
    if last:
        scratch.append(pltpu.VMEM((3 * group, both), F32))
    return pl.pallas_call(
        functools.partial(attention_kernel, steps=steps, first=first, last=last),
        grid_spec=pltpu.PrefetchScalarGridSpec(
            num_scalar_prefetch=1,
            grid=(steps,),
            in_specs=[
                whole,
                whole,
                whole,
            ]
            + [piece] * steps
            + ([] if first else [window]),
            out_specs=[piece] * steps
            + ([whole] * 3 if last else [window]),
            scratch_shapes=scratch,
        ),
        out_shape=[jax.ShapeDtypeStruct(out, BF16)] * steps
        + (
            [part, part, jax.ShapeDtypeStruct(own.shape, F32)]
            if last
            else [jax.ShapeDtypeStruct((3 * group, both), F32)]
        ),
        compiler_params=pltpu.CompilerParams(vmem_limit_bytes=20 << 20),
        cost_estimate=pl.CostEstimate(
            flops=7_500_000_000 * steps, bytes_accessed=2 << 20, transcendentals=1_200_000 * steps
        ),
        name="attention",
    )(*([place, far, near, own] + pieces + ([] if first else [before])))


def grad_hidden_kernel(place_ref, *refs):
    grads, weights, (o_ref, lined) = refs[:MEMBERS], refs[MEMBERS:-2], refs[-2:]
    _, half, width = weights[0].shape
    tok = o_ref.shape[1]
    for k, grad in enumerate(grads):
        to = place_ref[0] ^ k ^ place_ref[3]
        lined[to] = grad[...]
    line = jnp.concatenate([lined[k] for k in range(MEMBERS)], axis=1)
    for b in range(2 * MEMBERS):
        base = b // MEMBERS * MEMBERS
        rows = jnp.concatenate([weights[base + k][b % MEMBERS] for k in range(MEMBERS)], axis=1)
        total = nt(line, rows).astype(BF16)
        at = feature_block(place_ref, b // MEMBERS, b % MEMBERS) * half
        at = pl.ds(pl.multiple_of(at, half), half)
        for t in range(MEMBERS):
            o_ref[place_ref[0] ^ t, :, at] = total[t * tok : (t + 1) * tok]


def grad_hidden_quarter(place, pieces, weights):
    rows, width = pieces[0].shape
    half = weights[0].shape[1]
    depth = half * 2 * MEMBERS
    out = (MEMBERS, rows // MEMBERS, depth)
    return pl.pallas_call(
        grad_hidden_kernel,
        grid_spec=pltpu.PrefetchScalarGridSpec(
            num_scalar_prefetch=1,
            grid=(1,),
            in_specs=[pl.BlockSpec(pieces[0].shape, lambda i, p: (0, 0))] * MEMBERS
            + [pl.BlockSpec(weights[0].shape, lambda i, p: (0, 0, 0))] * len(weights),
            out_specs=pl.BlockSpec(out, lambda i, p: (0, 0, 0)),
            scratch_shapes=[pltpu.VMEM((MEMBERS, rows, width), BF16)],
        ),
        out_shape=jax.ShapeDtypeStruct(out, BF16),
        compiler_params=pltpu.CompilerParams(vmem_limit_bytes=32 << 20),
        cost_estimate=pl.CostEstimate(
            flops=2 * rows * depth * width * MEMBERS, bytes_accessed=8 << 20, transcendentals=0
        ),
        name="grad_hidden",
    )(place, *pieces, *weights)


def weight_grad_kernel(place_ref, h_ref, d0, d1, d2, d3, o_ref):
    xs, yhs, _, rows, cols = o_ref.shape
    for k, d in enumerate((d0, d1, d2, d3)):
        at = pl.multiple_of((place_ref[0] ^ k) * HEAD, HEAD)
        term = nn(h_ref[...], d[...]).astype(o_ref.dtype).reshape(xs, yhs, rows, 2 * HEAD)
        o_ref[:, :, 0, :, pl.ds(at, HEAD)] = term[..., :HEAD]
        o_ref[:, :, 0, :, pl.ds(cols // 2 + at, HEAD)] = term[..., HEAD:]


def weight_grad_share(place, turned, pieces, steps, dtype):
    feats, tokens = turned.shape
    both = pieces[0].shape[1]
    cols = both * KV_HEADS
    step = feats // (2 * steps)
    xs, yhs = lax.axis_size("x"), lax.axis_size("yh")
    out = (xs, yhs, steps, step // (xs * yhs), cols)
    return pl.pallas_call(
        weight_grad_kernel,
        grid_spec=pltpu.PrefetchScalarGridSpec(
            num_scalar_prefetch=1,
            grid=(steps,),
            in_specs=[pl.BlockSpec((step, tokens), lambda i, p: (p[1] * steps + i, 0))]
            + [pl.BlockSpec((tokens, both), lambda i, p: (0, 0))] * 4,
            out_specs=pl.BlockSpec((xs, yhs, 1) + out[3:], lambda i, p: (0, 0, i, 0, 0)),
        ),
        out_shape=jax.ShapeDtypeStruct(out, dtype),
        compiler_params=pltpu.CompilerParams(vmem_limit_bytes=14 << 20),
        cost_estimate=pl.CostEstimate(
            flops=feats * tokens * cols, bytes_accessed=5 << 20, transcendentals=0
        ),
        name="weight_grad",
    )(place, turned, *pieces)


def total_kernel(x_ref, o_ref):
    total = x_ref[0].astype(F32)
    for k in range(1, x_ref.shape[0]):
        total = total + x_ref[k].astype(F32)
    o_ref[...] = total.astype(o_ref.dtype)


def total(x, steps):
    count, blocks = x.shape[:2]
    size = blocks // steps
    tail = x.shape[2:]
    return small(
        "total",
        (steps,),
        [pl.BlockSpec((count, size) + tail, lambda i: (0, i, 0, 0))],
        pl.BlockSpec((size,) + tail, lambda i: (i, 0, 0)),
        jax.ShapeDtypeStruct((blocks,) + tail, x.dtype),
        total_kernel,
    )(x)


def merge_kernel(core_ref, mine_ref, theirs_ref, o_ref):
    @pl.when(pl.program_id(0) == core_ref[0])
    def _():
        o_ref[...] = mine_ref[...].astype(F32)

    @pl.when(pl.program_id(0) != core_ref[0])
    def _():
        o_ref[...] = theirs_ref[...].astype(F32)


def merge(core, mine, theirs):
    rows, cols = mine.shape
    block = pl.BlockSpec((rows, cols), lambda i, c: (0, 0))
    return small(
        "merge",
        (2,),
        [block, block],
        pl.BlockSpec((rows, cols), lambda i, c: (i, 0)),
        jax.ShapeDtypeStruct((2 * rows, cols), F32),
        merge_kernel,
        1,
    )(core, mine, theirs)


def body(hidden, kv_blocks, kv_scale, queries, grad_out):
    tok = hidden.shape[0]
    shard, kv_cols = kv_blocks.shape
    half = shard // 2
    zh = lax.axis_index("zh")
    core = lax.axis_index("core").reshape(1)
    member = lax.axis_index(GROUP).reshape(1)
    xs, zhs = lax.axis_size("x"), lax.axis_size("zh")

    x = lax.axis_index("x").reshape(1)
    place = jnp.concatenate([member, core, zh.reshape(1), x]).astype(jnp.int32)
    rows = dequantize(jnp.concatenate([core, x]), kv_blocks, kv_scale)
    rows, hidden, queries = lax.optimization_barrier((rows, hidden, queries))
    packed, pieces = pack_hidden(hidden, zhs), pack_heads(member, queries, grad_out)
    rows = jnp.stack([rows] + [swapped(rows, "zh", k) for k in range(1, zhs)])
    rows, packed, pieces = lax.optimization_barrier((rows, packed, pieces))
    weights = [rows] + [swapped(rows, "x", k) for k in range(1, xs)]
    quarter = exchange(packed, GROUP).reshape(MEMBERS * tok, -1)
    quarter, pieces, weights = lax.optimization_barrier((quarter, pieces, weights))
    weights += [swapped(w, "core", 1) for w in weights]

    partial = project(place, quarter, weights)
    partial = exchange(partial, GROUP)
    own = jnp.sum(partial, axis=0).astype(BF16)
    far = shifted(own, AXES, 2 * MEMBERS)
    near = shifted(own, AXES, MEMBERS)
    quarter, own = lax.optimization_barrier((quarter, own))
    turned = turn(quarter)
    far, near, turned, pieces = lax.optimization_barrier((far, near, turned, pieces))

    first = lax.axis_index(AXES) // MEMBERS * MEMBERS
    order = member ^ jnp.array([0, 3, 1, 2], jnp.int32)
    lim = jnp.maximum(0, SPAN - (first + order) * tok)

    def blocks(start, stop):
        return jnp.concatenate([order[start:stop], lim[start:stop]]).astype(jnp.int32)

    out0, before = attention(blocks(0, 1), [pieces[0]], far, near, own)
    head3 = swapped(pieces[3], GROUP, 3)
    before, head3, pieces = lax.optimization_barrier((before, head3, pieces))
    out3, before = attention(blocks(1, 2), [head3], far, near, own, before)
    head1, head2 = swapped(pieces[1], GROUP, 1), swapped(pieces[2], GROUP, 2)
    before, head1, head2, out3 = lax.optimization_barrier((before, head1, head2, out3))
    out3 = swapped(out3, GROUP, 3)
    out1, out2, dfar, dnear, down = attention(
        blocks(2, 4), [head1, head2], far, near, own, before, last=True
    )
    dfar, dnear, out3 = lax.optimization_barrier((dfar, dnear, out3))
    out1 = swapped(out1, GROUP, 1)
    from_far = shifted(dfar, AXES, -2 * MEMBERS)
    from_near = shifted(dnear, AXES, -MEMBERS)
    from_far, from_near, out1 = lax.optimization_barrier((from_far, from_near, out1))
    from_far, from_near = from_far.astype(F32), from_near.astype(F32)
    all_grad = (down + from_near + from_far).astype(BF16)
    inside = down + jnp.where(zh + 1 < zhs, from_near, 0.0) + jnp.where(zh + 2 < zhs, from_far, 0.0)
    seg_grad = inside.astype(BF16)
    grads = fanned(all_grad)

    theirs = weight_grad_share(jnp.concatenate([member, 1 - core]), turned, grads, zhs, BF16)
    mine = weight_grad_share(jnp.concatenate([member, core]), turned, grads, zhs, F32)

    seg_grad, grads = lax.optimization_barrier((seg_grad, grads))
    segs = fanned(seg_grad)
    mine = (mine + swapped(theirs, "core", 1).astype(F32)).astype(BF16)
    back = grad_hidden_quarter(place, segs, weights)
    parts = exchange(mine, "x")
    backs = dealt(back)
    out2 = swapped(out2, GROUP, 2)
    parts, out2, backs[:3] = lax.optimization_barrier((parts, out2, backs[:3]))
    parts = total(parts.reshape((xs, -1) + parts.shape[3:]), 4)
    parts = exchange(parts, ("yh", "zh"))
    summed = jnp.sum(parts.astype(F32), axis=0).astype(BF16)
    attn_out, grad_queries = unpack_heads(member, [out0, out1, out2, out3])
    attn_out, grad_queries, summed = lax.optimization_barrier((attn_out, grad_queries, summed))
    spread = jnp.broadcast_to(summed[None], (half // summed.shape[0],) + summed.shape)
    spread = exchange(spread, PLANE)
    backs, spread = lax.optimization_barrier((backs, spread))
    grad_hidden = unpack_hidden(member, backs, zhs)
    spread = spread.reshape(half, kv_cols)
    weight_grad = merge(core, spread, swapped(spread, "core", 1))
    return (attn_out, grad_queries, grad_hidden, weight_grad)


def solution(mesh):
    finer = Mesh(mesh.devices.reshape(SIZES), AXES)
    placed = (P(AXES, None), P(FSDP, None), P(FSDP, None), P(AXES, None), P(AXES, None))
    return jax.shard_map(
        body,
        mesh=finer,
        in_specs=placed,
        out_specs=(P(AXES, None), P(AXES, None), P(AXES, None), P(FSDP, None)),
        check_vma=False,
    )
```
